32 devices in a mesh: swath: 2 (over x), rng: 16 (over z, y, core).
Axes of the slice: x: 2, y: 2, z: 4, core: 2. Of those that a mesh axis runs over, the one named last changes fastest.
Arguments:
- echoes: float32 [2, 512, 32768], P(None, ('swath', 'rng')), parts along dimension 1, may hold values from -6 to 6
- doppler_filter: float32 [2, 32768], replicated, may hold values from -5 to 5
- migration_shift: int32 [32768], replicated, may hold values from 0 to 9, as said below
- kernel_index: int32 [32768], replicated, may hold values from 0 to 15
- kernel_taps: float32 [16, 16], replicated, may hold values from -1.5 to 1.5
Outputs:
- image: float32 [2, 512, 32768], P(None, ('swath', 'rng')), parts along dimension 1
The draws below stay inside these ranges and needn't reach their ends.
There are 2 independent parts, one for each index of `swath`. The reference program is written for one: setup_inputs(seed, part) draws one part's arguments, and reference() takes and returns one part's arrays. A program takes and returns all parts, laid end to end along the dimension named above; an argument that names none is the same for every part. Nothing has to cross between parts.
Inputs may be any that keep to these rules, and one draw needn't show every extreme that they name: `migration_shift`: both 0 and 9 occur.
All inputs are finite; a program needn't handle non-finite values.
Results may differ from the reference program's by a relative error of at most 0.0041.
Values may be sent and summed in bfloat16 or wider, within the bound.
A program may use at most 64 MiB of HBM per device.

```python
import math
import jax
import jax.numpy as jnp
from jax import lax

PULSES = 32768
RANGE = 256
TAPS = 16
NKER = 16
SMAX = 9


def draw_migration_shift(key, part):
    key_values, key_top, key_gap = jax.random.split(key, 3)
    values = jax.random.randint(key_values, (PULSES,), 0, SMAX + 1)
    where_top = jax.random.randint(key_top, (), 0, PULSES)
    distance = jax.random.randint(key_gap, (), 1, PULSES)
    where_zero = (where_top + distance) % PULSES
    positions = jnp.arange(PULSES, dtype=jnp.int32)
    values = jnp.where(positions == where_top, SMAX, values)
    return jnp.where(positions == where_zero, 0, values).astype(jnp.int32)


def place_ends(values, rng, low, top_value):
    shape = values.shape
    index_at = [jax.random.randint(jax.random.fold_in(rng, axis), (), 0, shape[axis]) for axis in range(len(shape))]
    values = values.at[tuple(index_at)].set(low)
    longest = shape.index(max(shape))
    index_at[longest] = (index_at[longest] + 1) % shape[longest]
    return values.at[tuple(index_at)].set(top_value)


def block_scale(stream_key, dims, shards, low, top_value):
    def one(axis_at, shards_of):
        draws = jax.random.uniform(jax.random.fold_in(jax.random.fold_in(stream_key, 6), axis_at), (shards_of,), jnp.float32, low / len(shards), top_value / len(shards))
        return jnp.repeat(jnp.exp(draws), dims[axis_at] // shards_of).reshape((-1,) + (1,) * (len(dims) - axis_at - 1))

    level = one(*shards[0])
    for cut in shards[1:]:
        level = level * one(*cut)
    return level


def normal_values(key, dims, deviation, limit, cuts=(), kind=jnp.bfloat16):
    values = jax.random.normal(key, dims, jnp.float32) * deviation
    if len(cuts) > 0:
        values = block_scale(key, dims, cuts, -0.22, 0.18) * values
    return jnp.clip(values, min=-limit, max=limit).astype(kind)


def setup_inputs(seed: int = 0, part: int = 0) -> dict:
    seeds = jax.random.split(jax.random.key(seed), 6)
    own_keys = jax.random.split(jax.random.fold_in(seeds[5], part), 6)
    echoes = normal_values(own_keys[0], (2, RANGE, PULSES), 1.0, 6.0, ((1, 16),), jnp.float32)
    doppler_filter = normal_values(seeds[1], (2, PULSES), 0.7, 5.0, (), jnp.float32)
    migration_shift = draw_migration_shift(jax.random.fold_in(seeds[5], 71), part)
    kernel_index = place_ends(jax.random.randint(seeds[3], (PULSES,), 0, NKER), jax.random.fold_in(seeds[3], 1), 0, NKER - 1).astype(jnp.int32)
    kernel_taps = normal_values(seeds[4], (NKER, TAPS), TAPS ** -0.5, 1.5, (), jnp.float32)
    return dict(echoes=echoes, doppler_filter=doppler_filter, migration_shift=migration_shift, kernel_index=kernel_index, kernel_taps=kernel_taps)


def reference(echoes, doppler_filter, migration_shift, kernel_index, kernel_taps):
    norm_scale = 1.0 / math.sqrt(PULSES)
    samples = lax.complex(echoes[0], echoes[1])
    spectrum = jnp.fft.fft(samples, axis=1) * norm_scale
    response = lax.complex(doppler_filter[0], -doppler_filter[1])
    weighted = spectrum * response[None, :]
    filtered = jnp.stack([jnp.real(weighted), jnp.imag(weighted)]).astype(jnp.bfloat16)
    coefficients = kernel_taps[kernel_index]
    tap_numbers = jnp.arange(TAPS, dtype=jnp.int32)
    low_margin = SMAX + TAPS // 2 - 1
    padded = jnp.pad(filtered, ((0, 0), (low_margin, TAPS // 2), (0, 0)))
    running = jnp.zeros((2, RANGE, PULSES), jnp.float32)
    for offset_slot in range(TAPS + SMAX):
        chosen = (tap_numbers[None, :] == (offset_slot - migration_shift)[:, None]).astype(jnp.float32)
        column_weight = lax.optimization_barrier(jnp.sum(coefficients * chosen, axis=1))
        first_row = low_margin + TAPS // 2 - offset_slot
        segment = padded[:, first_row:first_row + RANGE, :].astype(jnp.float32)
        running = running + column_weight[None, None, :] * segment
    migrated = running.astype(jnp.bfloat16)
    restored = lax.complex(migrated[0].astype(jnp.float32), migrated[1].astype(jnp.float32))
    image_parts = jnp.fft.ifft(restored, axis=1) / norm_scale
    return jnp.stack([jnp.real(image_parts), jnp.imag(image_parts)]).astype(jnp.float32)
```

```python
import functools
import math

import jax
import jax.numpy as jnp
import numpy as np
from jax import lax
from jax.experimental import pallas as pl
from jax.experimental.pallas import tpu as pltpu
from jax.sharding import PartitionSpec as P

F2 = 256
SMAX = 9
GROUP = 8
CHUNK = 16

f32 = jnp.float32
bf16 = jnp.bfloat16


MESH = pl.DeviceIdType.MESH


def dft(length):
    numbers = np.arange(length)
    angles = (numbers[:, None] * numbers[None, :] % length) * (2.0 * math.pi / length)
    return np.cos(angles), np.sin(angles)


def split(table):
    table = table.astype(np.float32)
    high = table.astype(bf16)
    return high, (table - high.astype(np.float32)).astype(bf16)


def twiddles(outer, inner):
    angles = (np.arange(outer)[:, None] * np.arange(inner)[None, :]) * (
        2.0 * math.pi / (outer * inner)
    )
    return np.stack([np.cos(angles), np.sin(angles)]).astype(np.float32)


def dot(a, b):
    return jnp.dot(a, b, preferred_element_type=f32)


def halves(value):
    high = value.astype(bf16)
    return high, (value - high.astype(f32)).astype(bf16)


def main_kernel(
    count, outer, inner, taps,
    x_hbm, w1h_ref, w1l_ref, w2h_ref, w2l_ref, t_ref, v2_ref, h_ref, s_in, k_in, taps_ref,
    y_hbm,
    x_buf, hr_ref, hi_ref, s_ref, k_ref, tab_ref, own, prev, nxt, low, mix, m_ref, y_buf,
    xsem, ysem, ssem, rsem,
):
    me = lax.axis_index("rng")
    role = me % 4
    first = me < 4
    final = me >= count - 4
    lanes = 128
    parts = inner // lanes
    stride = GROUP * parts
    chunks = outer // CHUNK
    rows = 2 * GROUP
    lead = jnp.where(role == 0, 0, jnp.where(role == 2, 0, 1))

    def fetch(g):
        return pltpu.make_async_copy(x_hbm.at[:, g], x_buf.at[:, g], xsem.at[g])

    fetch(lead).start()
    fetch(1 - lead).start()

    barrier = pltpu.get_barrier_semaphore()

    def greet(target):
        pl.semaphore_signal(barrier, inc=1, device_id={"rng": target}, device_id_type=MESH)

    @pl.when(role == 0)
    def _():
        greet(me + 1)

        @pl.when(jnp.logical_not(first))
        def _():
            greet(me - 1)
            greet(me - 3)

    @pl.when(role == 1)
    def _():
        greet(me - 1)
        greet(me + 1)

        @pl.when(jnp.logical_not(final))
        def _():
            greet(me + 3)

    @pl.when(role == 2)
    def _():
        greet(me - 1)
        greet(me + 1)

    @pl.when(role == 3)
    def _():
        greet(me - 1)

        @pl.when(jnp.logical_not(final))
        def _():
            greet(me + 1)

    norm = 1.0 / math.sqrt(outer * inner)
    hr_ref[...] = h_ref[pl.ds(0, inner, stride=2), :].T * norm
    hi_ref[...] = h_ref[pl.ds(1, inner, stride=2), :].T * norm

    def forward(g, q):
        w1h = w1h_ref[...]
        w1l = w1l_ref[...]
        ah, al = [], []
        for j in range(2):
            r = q * 2 + j
            columns = []
            for c in range(2):
                columns.append(
                    jnp.concatenate(
                        [
                            x_buf[c, g, pl.ds(h * GROUP + r, outer, stride=stride), :]
                            for h in range(parts)
                        ],
                        axis=1,
                    )
                )
            xh, xl = halves(jnp.concatenate(columns, axis=0))
            s = dot(w1h, xh) + dot(w1h, xl) + dot(w1l, xh)
            re, im = s[:outer], s[outer:]
            tc, ts = t_ref[0], t_ref[1]
            a, b = halves(jnp.concatenate([re * tc + im * ts, im * tc - re * ts], axis=1))
            ah.append(a)
            al.append(b)
        rh = jnp.concatenate(ah, axis=0)
        rl = jnp.concatenate(al, axis=0)
        z = dot(rh, w2h_ref[...]) + dot(rh, w2l_ref[...]) + dot(rl, w2h_ref[...])
        hr, hi = hr_ref[...], hi_ref[...]
        for j in range(2):
            re = z[j * outer : (j + 1) * outer, :inner]
            im = z[j * outer : (j + 1) * outer, inner:]
            own[g, :, 0, q * 2 + j] = (re * hr + im * hi).astype(bf16).reshape(chunks, CHUNK, inner)
            own[g, :, 1, q * 2 + j] = (im * hr - re * hi).astype(bf16).reshape(chunks, CHUNK, inner)

    def copy(kind, slot, src, dst, target):
        return pltpu.make_async_remote_copy(
            src_ref=src,
            dst_ref=dst,
            send_sem=ssem.at[kind, slot],
            recv_sem=rsem.at[kind, slot],
            device_id={"rng": target},
            device_id_type=MESH,
        )

    def pair(ref, g, q):
        return ref.at[g, :, :, pl.ds(q * 2, 2)]

    def a_pair(g, q):
        return copy(0, g * 4 + q, pair(own, g, q), pair(prev, g, q), (me + 1) % count)

    def b_pair(q):
        return copy(1, q, pair(own, 1, q), pair(prev, 1, q), (me + 1) % count)

    def c_pair(q):
        return copy(1, q, pair(own, 1, q), pair(prev, 1, q), (me + 1) % count)

    def up(c):
        return copy(2, c, own.at[0, c], nxt.at[c], (me + count - 1) % count)

    def far_up(c):
        return copy(3, c, own.at[0, c], low.at[c], (me + count - 3) % count)

    def mix_down(c):
        return copy(4, c, mix.at[c], prev.at[0, c], (me + 1) % count)

    def mix_up(c):
        return copy(5, c, mix.at[c], nxt.at[c], (me + count - 1) % count)

    def relay_down(c):
        return copy(6, c, nxt.at[c], prev.at[0, c], (me + 3) % count)

    def relay_up(c):
        return copy(7, c, prev.at[0, c], nxt.at[c], (me + 1) % count)

    fetch(lead).wait()

    def step(i, _):
        g = jnp.where(i < 4, lead, 1 - lead)
        q = i % 4

        @pl.when(i == 4)
        def _():
            fetch(1 - lead).wait()

        forward(g, q)

        @pl.when(i == 0)
        def _():
            middle = jnp.where(role == 0, jnp.logical_not(first), jnp.where(role == 1, jnp.logical_not(final), False))

            @pl.when(middle)
            def _():
                pl.semaphore_wait(barrier, 3)

            @pl.when(jnp.logical_not(middle) & ((role == 1) | (role == 2) | ((role == 3) & jnp.logical_not(final))))
            def _():
                pl.semaphore_wait(barrier, 2)

            @pl.when(jnp.logical_not(middle) & ((role == 0) | ((role == 3) & final)))
            def _():
                pl.semaphore_wait(barrier, 1)

        @pl.when((role == 0) | (role == 2))
        def _():
            a_pair(g, q).start()

        @pl.when((g == 1) & (role == 1))
        def _():
            b_pair(q).start()

        @pl.when((g == 1) & (role == 3) & jnp.logical_not(final))
        def _():
            c_pair(q).start()

        @pl.when((g == 0) & (q == 3) & (role == 0) & jnp.logical_not(first))
        def _():
            for c in range(chunks):
                far_up(c).start()

        @pl.when((g == 0) & (q == 3) & ((role == 1) | (role == 3)))
        def _():
            for c in range(chunks):
                up(c).start()

        return 0

    lax.fori_loop(0, 8, step, 0)
    s_ref[...] = s_in[...].T
    k_ref[...] = k_in[...].T
    padded = jnp.concatenate([taps_ref[...], jnp.zeros((taps_ref.shape[0], lanes - taps), f32)], axis=1)
    padded = jnp.concatenate([padded, jnp.zeros((lanes - taps_ref.shape[0], lanes), f32)], axis=0)
    tab_ref[...] = padded.T[:taps]

    def merge(c, high, lower):
        limit = SMAX - s_ref[pl.ds(pl.multiple_of(c * CHUNK, CHUNK), CHUNK), :]
        for d in range(2):
            for j in range(GROUP):
                mix[c, d, j] = jnp.where(
                    limit <= j, high[c, d, j].astype(f32), lower[c, d, j].astype(f32)
                ).astype(bf16)

    def send_mix(c):
        @pl.when(jnp.logical_not(final))
        def _():
            far_up(c).wait_recv()

        merge(c, own.at[0], low)
        mix_down(c).start()

    @pl.when((role == 0) & first)
    def _():
        prev[...] = jnp.zeros_like(prev)

    @pl.when((role == 1) & final)
    def _():
        low[...] = jnp.zeros_like(low)

    ahead = 4

    @pl.when((role == 0) & jnp.logical_not(first))
    def _():
        for q in range(4):
            c_pair(q).wait_recv()

    @pl.when(role == 1)
    def _():
        def head(c, _):
            send_mix(c)
            return 0

        lax.fori_loop(0, ahead, head, 0)

    @pl.when((role == 1) | (role == 3))
    def _():
        for n in range(8):
            a_pair(n // 4, n % 4).wait_recv()

    @pl.when(role == 2)
    def _():
        def head(c, _):
            up(c).wait_recv()
            merge(c, nxt, own.at[0])
            mix_up(c).start()
            return 0

        lax.fori_loop(0, chunks, head, 0)
        for q in range(4):
            b_pair(q).wait_recv()

    def out(c):
        return pltpu.make_async_copy(
            y_buf.at[c % 2],
            y_hbm.at[:, :, pl.ds(pl.multiple_of(c * CHUNK, CHUNK), CHUNK), :],
            ysem.at[c % 2],
        )

    def migrate(c):
        base = pl.multiple_of(c * CHUNK, CHUNK)
        for sub in range(CHUNK // 8):
            for part in range(parts):
                a = slice(sub * 8, sub * 8 + 8)
                b = slice(part * lanes, part * lanes + lanes)
                offset = SMAX - s_ref[pl.ds(base + sub * 8, 8), b]
                which = k_ref[pl.ds(base + sub * 8, 8), b]
                bits = [(offset & bit) != 0 for bit in (8, 4, 2, 1)]
                weights = [
                    jnp.take_along_axis(jnp.broadcast_to(tab_ref[k : k + 1, :], (8, 128)), which, axis=1, mode="promise_in_bounds")
                    for k in range(taps)
                ]
                for d in range(2):
                    line = [prev[g, c, d, i, a, b] for g in range(2) for i in range(GROUP)]
                    line += [own[g, c, d, i, a, b] for g in range(2) for i in range(GROUP)]
                    line += [nxt[c, d, i, a, b] for i in range(GROUP)]
                    line = [v.astype(f32) for v in line]
                    need = rows + taps - 1
                    for n, bit in enumerate((8, 4, 2, 1)):
                        keep = need + (bit - 1)
                        line = [
                            jnp.where(bits[n], line[j + bit], line[j]) if j + bit < len(line) else line[j]
                            for j in range(keep)
                        ]
                    for i in range(rows):
                        total = weights[0] * line[i + taps - 1]
                        for k in range(1, taps):
                            total = total + weights[k] * line[i + taps - 1 - k]
                        m_ref[i, a, d * inner + part * lanes : d * inner + part * lanes + lanes] = total
        flat = m_ref[...].reshape(rows * CHUNK, 2 * inner).astype(bf16)
        z = dot(flat, v2_ref[...]).reshape(rows, CHUNK, 2 * inner)
        re, im = z[:, :, :inner], z[:, :, inner:]
        tc, ts = t_ref[0, pl.ds(base, CHUNK), :][None], t_ref[1, pl.ds(base, CHUNK), :][None]

        @pl.when(c >= 2)
        def _():
            out(c - 2).wait()

        y_buf[c % 2, :, 0] = (re * tc - im * ts).astype(bf16)
        y_buf[c % 2, :, 1] = (re * ts + im * tc).astype(bf16)
        out(c).start()

    def work(c, _):
        @pl.when(role == 0)
        def _():
            up(c).wait_recv()

            @pl.when(jnp.logical_not(first))
            def _():
                relay_down(c).wait_recv()

        @pl.when(role == 1)
        def _():
            @pl.when(c + ahead < chunks)
            def _():
                send_mix(c + ahead)

            mix_up(c).wait_recv()

            @pl.when(jnp.logical_not(final))
            def _():
                relay_down(c).start()

        @pl.when(role == 2)
        def _():
            mix_down(c).wait_recv()
            relay_up(c).start()

        @pl.when(role == 3)
        def _():
            relay_up(c).wait_recv()

        migrate(c)
        return 0

    lax.fori_loop(0, chunks, work, 0)
    out(chunks - 2).wait()
    out(chunks - 1).wait()

    @pl.when((role == 0) | (role == 2))
    def _():
        for n in range(8):
            a_pair(n // 4, n % 4).wait_send()

    @pl.when((role == 0) & jnp.logical_not(first))
    def _():
        for c in range(chunks):
            far_up(c).wait_send()

    @pl.when((role == 1) | (role == 3))
    def _():
        for c in range(chunks):
            up(c).wait_send()

    @pl.when((role == 1) | ((role == 3) & jnp.logical_not(final)))
    def _():
        for q in range(4):
            b_pair(q).wait_send()

    @pl.when(role == 1)
    def _():
        for c in range(chunks):
            mix_down(c).wait_send()

        @pl.when(jnp.logical_not(final))
        def _():
            for c in range(chunks):
                relay_down(c).wait_send()

    @pl.when(role == 2)
    def _():
        for c in range(chunks):
            mix_up(c).wait_send()
            relay_up(c).wait_send()


def last_kernel(outer, inner, v1_ref, y_ref, o_ref):
    lanes = 128
    parts = inner // lanes
    stride = GROUP * parts
    scale = 1.0 / math.sqrt(outer * inner)
    for r in range(GROUP):
        z = dot(v1_ref[...], y_ref[r].reshape(2 * outer, inner)) * scale
        for c in range(2):
            for h in range(parts):
                o_ref[c, 0, pl.ds(h * GROUP + r, outer, stride=stride), :] = z[
                    c * outer : (c + 1) * outer, h * lanes : (h + 1) * lanes
                ]


def per_device(echoes, doppler_filter, migration_shift, kernel_index, kernel_taps):
    rows = echoes.shape[1]
    pulses = echoes.shape[2]
    inner = F2
    outer = pulses // inner
    taps = kernel_taps.shape[1]
    groups = rows // GROUP
    tiles = pulses // 128
    chunks = outer // CHUNK
    count = lax.axis_size("rng")
    assert groups == 2 and count % 4 == 0
    whole = lambda *shape: pl.BlockSpec(shape, lambda i: (0,) * len(shape))

    oc, osn = dft(outer)
    ic, isn = dft(inner)
    w1h, w1l = split(np.block([[oc, osn], [-osn, oc]]))
    w2h, w2l = split(np.block([[ic, -isn], [isn, ic]]))
    v2 = split(np.block([[ic, isn], [-isn, ic]]))[0]
    v1 = split(np.block([[oc, -osn], [osn, oc]]))[0]
    twist = twiddles(outer, inner)
    signal = (
        echoes.reshape(2, groups, GROUP, tiles, 128)
        .transpose(0, 1, 3, 2, 4)
        .reshape(2, groups, tiles * GROUP, 128)
    )
    response = doppler_filter.reshape(2, inner, outer).transpose(1, 0, 2).reshape(2 * inner, outer)
    anywhere = pl.BlockSpec(memory_space=pl.ANY)
    vmem = pl.BlockSpec(memory_space=pltpu.VMEM)
    piece = (2, GROUP, CHUNK, inner)
    y = pl.pallas_call(
        functools.partial(main_kernel, count, outer, inner, taps),
        in_specs=[anywhere] + [vmem] * 10,
        out_specs=anywhere,
        out_shape=jax.ShapeDtypeStruct((rows, 2, outer, inner), bf16),
        scratch_shapes=[
            pltpu.VMEM(signal.shape, f32),
            pltpu.VMEM((outer, inner), f32),
            pltpu.VMEM((outer, inner), f32),
            pltpu.VMEM((outer, inner), jnp.int32),
            pltpu.VMEM((outer, inner), jnp.int32),
            pltpu.VMEM((taps, 128), f32),
            pltpu.VMEM((groups, chunks) + piece, bf16),
            pltpu.VMEM((groups, chunks) + piece, bf16),
            pltpu.VMEM((chunks,) + piece, bf16),
            pltpu.VMEM((chunks,) + piece, bf16),
            pltpu.VMEM((chunks,) + piece, bf16),
            pltpu.VMEM((rows, CHUNK, 2 * inner), f32),
            pltpu.VMEM((2, rows, 2, CHUNK, inner), bf16),
            pltpu.SemaphoreType.DMA((2,)),
            pltpu.SemaphoreType.DMA((2,)),
            pltpu.SemaphoreType.DMA((8, 8)),
            pltpu.SemaphoreType.DMA((8, 8)),
        ],
        compiler_params=pltpu.CompilerParams(
            collective_id=0, has_side_effects=True, vmem_limit_bytes=48 << 20
        ),
        name="main",
    )(
        signal, jnp.asarray(w1h), jnp.asarray(w1l), jnp.asarray(w2h), jnp.asarray(w2l),
        jnp.asarray(twist), jnp.asarray(v2), response,
        migration_shift.reshape(inner, outer), kernel_index.reshape(inner, outer), kernel_taps,
    )
    image = pl.pallas_call(
        functools.partial(last_kernel, outer, inner),
        grid=(groups,),
        in_specs=[
            whole(*v1.shape),
            pl.BlockSpec((GROUP, 2, outer, inner), lambda i: (i, 0, 0, 0)),
        ],
        out_specs=pl.BlockSpec((2, 1, tiles * GROUP, 128), lambda i: (0, i, 0, 0)),
        out_shape=jax.ShapeDtypeStruct((2, groups, tiles * GROUP, 128), f32),
        name="last",
    )(jnp.asarray(v1), y)
    return (
        image.reshape(2, groups, tiles, GROUP, 128)
        .transpose(0, 1, 3, 2, 4)
        .reshape(2, rows, pulses)
    )


def solution(mesh):
    return jax.shard_map(
        per_device,
        mesh=mesh,
        in_specs=(P(None, ("swath", "rng"), None), P(), P(), P(), P()),
        out_specs=P(None, ("swath", "rng"), None),
        check_vma=False,
    )
```

```python
import functools
import math

import jax
import jax.numpy as jnp
import numpy as np
from jax import lax
from jax.experimental import pallas as pl
from jax.experimental.pallas import tpu as pltpu
from jax.sharding import PartitionSpec as P

F2 = 256
SMAX = 9
GROUP = 8
CHUNK = 16

f32 = jnp.float32
bf16 = jnp.bfloat16


MESH = pl.DeviceIdType.MESH


def dft(length):
    numbers = np.arange(length)
    angles = (numbers[:, None] * numbers[None, :] % length) * (2.0 * math.pi / length)
    return np.cos(angles), np.sin(angles)


def split(table):
    table = table.astype(np.float32)
    high = table.astype(bf16)
    return high, (table - high.astype(np.float32)).astype(bf16)


def twiddles(outer, inner):
    angles = (np.arange(outer)[:, None] * np.arange(inner)[None, :]) * (
        2.0 * math.pi / (outer * inner)
    )
    return np.stack([np.cos(angles), np.sin(angles)]).astype(np.float32)


def dot(a, b):
    return jnp.dot(a, b, preferred_element_type=f32)


def halves(value):
    high = value.astype(bf16)
    return high, (value - high.astype(f32)).astype(bf16)


def main_kernel(
    count, outer, inner, taps,
    x_hbm, w1_hbm, w2_hbm, t_hbm, h_hbm, v2_hbm, v1_hbm, s_hbm, k_hbm, taps_hbm,
    y_ref, v1_ref,
    x_buf, w1_ref, w2_ref, t_ref, h_ref, v2_ref, s_in, k_in, taps_ref,
    hr_ref, hi_ref, s_ref, k_ref, tab_ref, own, prev, nxt, low, mix, far, m_ref,
    xsem, tsem, ssem, rsem,
):
    me = lax.axis_index("rng")
    role = me % 4
    first = me < 4
    final = me >= count - 4
    lanes = 128
    parts = inner // lanes
    stride = GROUP * parts
    chunks = outer // CHUNK
    rows = 2 * GROUP
    lead = jnp.where(role == 0, 0, jnp.where(role == 2, 0, 1))

    def fetch(g):
        return pltpu.make_async_copy(x_hbm.at[:, g], x_buf.at[:, g], xsem.at[g])

    tables = [
        pltpu.make_async_copy(src, dst, tsem.at[n])
        for n, (src, dst) in enumerate(
            (
                (h_hbm, h_ref),
                (w1_hbm, w1_ref),
                (t_hbm, t_ref),
                (w2_hbm, w2_ref),
                (s_hbm, s_in),
                (k_hbm, k_in),
                (taps_hbm, taps_ref),
                (v2_hbm, v2_ref),
                (v1_hbm, v1_ref),
            )
        )
    ]
    tables[0].start()
    fetch(lead).start()
    for n in (1, 2, 3):
        tables[n].start()

    barrier = pltpu.get_barrier_semaphore()

    def greet(target):
        pl.semaphore_signal(barrier, inc=1, device_id={"rng": target}, device_id_type=MESH)

    @pl.when(role == 0)
    def _():
        greet(me + 1)

        @pl.when(jnp.logical_not(first))
        def _():
            greet(me - 1)
            greet(me - 3)

    @pl.when(role == 1)
    def _():
        greet(me - 1)
        greet(me + 1)

        @pl.when(jnp.logical_not(final))
        def _():
            greet(me + 2)
            greet(me + 3)

    @pl.when(role == 2)
    def _():
        greet(me - 1)
        greet(me + 1)

    @pl.when(role == 3)
    def _():
        greet(me - 1)

        @pl.when(jnp.logical_not(final))
        def _():
            greet(me - 2)
            greet(me + 1)

    norm = 1.0 / math.sqrt(outer * inner)
    tables[0].wait()
    for e in range(2):
        here = pl.ds(e * lanes, lanes)
        hr_ref[:, here] = h_ref[pl.ds(e * 2, lanes, stride=4), :].T * norm
        hi_ref[:, here] = h_ref[pl.ds(e * 2 + 1, lanes, stride=4), :].T * norm
    for n in (1, 2, 3):
        tables[n].wait()

    def forward(g, q):
        sums = [([], []), ([], [])]
        for j in range(2):
            r = q * 2 + j
            columns = []
            for c in range(2):
                columns.append(
                    jnp.concatenate(
                        [
                            x_buf[c, g, pl.ds(h * GROUP + r, outer, stride=stride), :]
                            for h in range(parts)
                        ],
                        axis=1,
                    )
                )
            xh, xl = halves(jnp.concatenate(columns, axis=0))
            both = dot(w1_ref[...], xh)
            s = both[: 2 * outer] + dot(w1_ref[: 2 * outer, :], xl) + both[2 * outer :]
            re, im = s[:outer], s[outer:]
            tc, ts = t_ref[0], t_ref[1]
            re, im = re * tc + im * ts, im * tc - re * ts
            left = jnp.concatenate([re[:, :lanes], im[:, :lanes]], axis=1)
            right = jnp.concatenate([re[:, lanes:], im[:, lanes:]], axis=1)
            for e, value in enumerate((left + right, left - right)):
                a, b = halves(value)
                sums[e][0].append(a)
                sums[e][1].append(b)
        for e in range(2):
            both = dot(jnp.concatenate(sums[e][0] + sums[e][1], axis=0), w2_ref[0, e])
            high = jnp.concatenate(sums[e][0], axis=0)
            z = both[: 2 * outer] + dot(high, w2_ref[1, e]) + both[2 * outer :]
            here = pl.ds(e * lanes, lanes)
            hr, hi = hr_ref[:, here], hi_ref[:, here]
            for j in range(2):
                re = z[j * outer : (j + 1) * outer, :lanes]
                im = z[j * outer : (j + 1) * outer, lanes:]
                own[g, :, 0, q * 2 + j, :, here] = (re * hr + im * hi).astype(bf16).reshape(chunks, CHUNK, lanes)
                own[g, :, 1, q * 2 + j, :, here] = (im * hr - re * hi).astype(bf16).reshape(chunks, CHUNK, lanes)

    def copy(kind, slot, src, dst, target):
        return pltpu.make_async_remote_copy(
            src_ref=src,
            dst_ref=dst,
            send_sem=ssem.at[kind, slot],
            recv_sem=rsem.at[kind, slot],
            device_id={"rng": target},
            device_id_type=MESH,
        )

    def pair(ref, g, q):
        return ref.at[g, :, :, pl.ds(q * 2, 2)]

    def a_pair(g, q):
        return copy(0, g * 4 + q, pair(own, g, q), pair(prev, g, q), (me + 1) % count)

    def b_pair(q):
        return copy(1, q, pair(own, 1, q), pair(prev, 1, q), (me + 1) % count)

    def c_pair(q):
        return copy(1, q, pair(own, 1, q), pair(prev, 1, q), (me + 1) % count)

    def away(q):
        return copy(1, 4 + q, pair(own, 1, q), far.at[q], (me + count - 2) % count)

    def onward(q):
        return pltpu.make_async_remote_copy(
            src_ref=far.at[q],
            dst_ref=pair(prev, 1, q),
            send_sem=ssem.at[8, q],
            recv_sem=rsem.at[1, q],
            device_id={"rng": (me + 3) % count},
            device_id_type=MESH,
        )

    def up(c):
        return copy(2, c, own.at[0, c], nxt.at[c], (me + count - 1) % count)

    def far_up(c):
        return copy(3, c, own.at[0, c], low.at[c], (me + count - 3) % count)

    def mix_down(c):
        return copy(4, c, mix.at[c], prev.at[0, c], (me + 1) % count)

    def mix_up(c):
        return copy(5, c, mix.at[c], nxt.at[c], (me + count - 1) % count)

    def relay_down(c):
        return copy(6, c, nxt.at[c], prev.at[0, c], (me + 3) % count)

    def relay_up(c):
        return copy(7, c, prev.at[0, c], nxt.at[c], (me + 1) % count)

    layers = count // 4
    detour = 4 - (4 * (me // 4 + 1) + layers - 1) // layers
    fetch(lead).wait()
    fetch(1 - lead).start()
    for n in range(4, 9):
        tables[n].start()

    def step(i, _):
        g = jnp.where(i < 4, lead, 1 - lead)
        q = i % 4

        @pl.when(i == 4)
        def _():
            fetch(1 - lead).wait()

        forward(g, q)

        @pl.when(i == 0)
        def _():
            for amount, here in (
                (1, ((role == 0) & first) | ((role == 3) & final)),
                (2, (role == 2) | ((role == 1) & final)),
                (3, ((role == 0) & jnp.logical_not(first)) | ((role == 3) & jnp.logical_not(final))),
                (4, (role == 1) & jnp.logical_not(final)),
            ):

                @pl.when(here)
                def _():
                    pl.semaphore_wait(barrier, amount)

        @pl.when((role == 0) | (role == 2))
        def _():
            a_pair(g, q).start()

        @pl.when((g == 1) & (role == 1))
        def _():
            b_pair(q).start()

        @pl.when((g == 1) & (role == 3) & jnp.logical_not(final))
        def _():
            @pl.when(q < detour)
            def _():
                away(q).start()

            @pl.when(q >= detour)
            def _():
                c_pair(q).start()

        @pl.when((g == 0) & (q == 3) & (role == 0) & jnp.logical_not(first))
        def _():
            for c in range(chunks):
                far_up(c).start()

        @pl.when((g == 0) & (q == 3) & ((role == 1) | (role == 3)))
        def _():
            for c in range(chunks):
                up(c).start()

        return 0

    lax.fori_loop(0, 8, step, 0)
    for n in range(4, 9):
        tables[n].wait()
    for e in range(2):
        here = pl.ds(e * lanes, lanes)
        s_ref[:, here] = s_in[pl.ds(e, lanes, stride=2), :].T
        k_ref[:, here] = k_in[pl.ds(e, lanes, stride=2), :].T
    padded = jnp.concatenate([taps_ref[...], jnp.zeros((taps_ref.shape[0], lanes - taps), f32)], axis=1)
    padded = jnp.concatenate([padded, jnp.zeros((lanes - taps_ref.shape[0], lanes), f32)], axis=0)
    tab_ref[...] = padded.T[:taps]

    def merge(c, high, lower):
        limit = SMAX - s_ref[pl.ds(pl.multiple_of(c * CHUNK, CHUNK), CHUNK), :]
        for d in range(2):
            for j in range(GROUP):
                mix[c, d, j] = jnp.where(
                    limit <= j, high[c, d, j].astype(f32), lower[c, d, j].astype(f32)
                ).astype(bf16)

    def send_mix(c):
        @pl.when(jnp.logical_not(final))
        def _():
            far_up(c).wait_recv()

        merge(c, own.at[0], low)
        mix_down(c).start()

    @pl.when((role == 0) & first)
    def _():
        prev[...] = jnp.zeros_like(prev)

    @pl.when((role == 1) & final)
    def _():
        low[...] = jnp.zeros_like(low)

    ahead = 4

    @pl.when((role == 0) & jnp.logical_not(first))
    def _():
        for q in range(4):
            c_pair(q).wait_recv()

    @pl.when((role == 1) & jnp.logical_not(final))
    def _():
        for q in range(4):

            @pl.when(q < detour)
            def _():
                away(q).wait_recv()
                onward(q).start()

    @pl.when(role == 1)
    def _():
        def head(c, _):
            send_mix(c)
            return 0

        lax.fori_loop(0, ahead, head, 0)

    @pl.when((role == 1) | (role == 3))
    def _():
        for n in range(8):
            a_pair(n // 4, n % 4).wait_recv()

    @pl.when(role == 2)
    def _():
        def head(c, _):
            up(c).wait_recv()
            merge(c, nxt, own.at[0])
            mix_up(c).start()
            return 0

        lax.fori_loop(0, chunks, head, 0)
        for q in range(4):
            b_pair(q).wait_recv()

    def migrate(c):
        base = pl.multiple_of(c * CHUNK, CHUNK)
        for sub in range(CHUNK // 8):
            for part in range(parts):
                a = slice(sub * 8, sub * 8 + 8)
                b = slice(part * lanes, part * lanes + lanes)
                offset = SMAX - s_ref[pl.ds(base + sub * 8, 8), b]
                which = k_ref[pl.ds(base + sub * 8, 8), b]
                bits = [(offset & bit) != 0 for bit in (8, 4, 2, 1)]
                weights = [
                    jnp.take_along_axis(jnp.broadcast_to(tab_ref[k : k + 1, :], (8, 128)), which, axis=1, mode="promise_in_bounds")
                    for k in range(taps)
                ]
                for d in range(2):
                    line = [prev[g, c, d, i, a, b] for g in range(2) for i in range(GROUP)]
                    line += [own[g, c, d, i, a, b] for g in range(2) for i in range(GROUP)]
                    line += [nxt[c, d, i, a, b] for i in range(GROUP)]
                    line = [v.astype(f32) for v in line]
                    need = rows + taps - 1
                    for n, bit in enumerate((8, 4, 2, 1)):
                        keep = need + (bit - 1)
                        line = [
                            jnp.where(bits[n], line[j + bit], line[j]) if j + bit < len(line) else line[j]
                            for j in range(keep)
                        ]
                    for i in range(rows):
                        total = weights[0] * line[i + taps - 1]
                        for k in range(1, taps):
                            total = total + weights[k] * line[i + taps - 1 - k]
                        m_ref[i, a, part * inner + d * lanes : part * inner + d * lanes + lanes] = total
        flat = m_ref[...].reshape(rows * CHUNK, 2 * inner).astype(bf16)
        even = dot(flat[:, :inner], v2_ref[0])
        odd = dot(flat[:, inner:], v2_ref[1])
        here = pl.ds(base, CHUNK)
        for n, z in enumerate((even + odd, even - odd)):
            z = z.reshape(rows, CHUNK, inner)
            re, im = z[:, :, :lanes], z[:, :, lanes:]
            half = pl.ds(n * lanes, lanes)
            tc, ts = (t_ref[0, here, half] * norm)[None], (t_ref[1, here, half] * norm)[None]
            y_ref[:, 0, here, half] = (re * tc - im * ts).astype(bf16)
            y_ref[:, 1, here, half] = (re * ts + im * tc).astype(bf16)

    def work(c, _):
        @pl.when(role == 0)
        def _():
            up(c).wait_recv()

            @pl.when(jnp.logical_not(first))
            def _():
                relay_down(c).wait_recv()

        @pl.when(role == 1)
        def _():
            @pl.when(c + ahead < chunks)
            def _():
                send_mix(c + ahead)

            mix_up(c).wait_recv()

            @pl.when(jnp.logical_not(final))
            def _():
                relay_down(c).start()

        @pl.when(role == 2)
        def _():
            mix_down(c).wait_recv()
            relay_up(c).start()

        @pl.when(role == 3)
        def _():
            relay_up(c).wait_recv()

        migrate(c)
        return 0

    lax.fori_loop(0, chunks, work, 0)

    @pl.when((role == 0) | (role == 2))
    def _():
        for n in range(8):
            a_pair(n // 4, n % 4).wait_send()

    @pl.when((role == 0) & jnp.logical_not(first))
    def _():
        for c in range(chunks):
            far_up(c).wait_send()

    @pl.when((role == 1) | (role == 3))
    def _():
        for c in range(chunks):
            up(c).wait_send()

    @pl.when((role == 3) & jnp.logical_not(final))
    def _():
        for q in range(4):

            @pl.when(q < detour)
            def _():
                away(q).wait_send()

            @pl.when(q >= detour)
            def _():
                c_pair(q).wait_send()

    @pl.when((role == 1) & jnp.logical_not(final))
    def _():
        for q in range(4):

            @pl.when(q < detour)
            def _():
                onward(q).wait_send()

    @pl.when(role == 1)
    def _():
        for q in range(4):
            b_pair(q).wait_send()
        for c in range(chunks):
            mix_down(c).wait_send()

        @pl.when(jnp.logical_not(final))
        def _():
            for c in range(chunks):
                relay_down(c).wait_send()

    @pl.when(role == 2)
    def _():
        for c in range(chunks):
            mix_up(c).wait_send()
            relay_up(c).wait_send()


def last_kernel(outer, inner, v1_ref, y_ref, o_hbm, o_buf, sem):
    lanes = 128
    parts = inner // lanes
    stride = GROUP * parts
    groups = y_ref.shape[0] // GROUP
    outs = [pltpu.make_async_copy(o_buf.at[:, g], o_hbm.at[:, g], sem.at[g]) for g in range(groups)]
    for g in range(groups):
        for r in range(GROUP):
            z = dot(v1_ref[...], y_ref[g * GROUP + r].reshape(2 * outer, inner))
            for c in range(2):
                for h in range(parts):
                    o_buf[c, g, pl.ds(h * GROUP + r, outer, stride=stride), :] = z[
                        c * outer : (c + 1) * outer, h * lanes : (h + 1) * lanes
                    ]
        outs[g].start()
    for out in outs:
        out.wait()


def per_device(echoes, doppler_filter, migration_shift, kernel_index, kernel_taps):
    rows = echoes.shape[1]
    pulses = echoes.shape[2]
    inner = F2
    outer = pulses // inner
    taps = kernel_taps.shape[1]
    groups = rows // GROUP
    tiles = pulses // 128
    chunks = outer // CHUNK
    count = lax.axis_size("rng")
    assert groups == 2 and count % 4 == 0
    half = inner // 2
    oc, osn = dft(outer)
    w1 = np.concatenate(split(np.block([[oc, osn], [-osn, oc]])))
    angles = np.arange(half)[:, None] * np.arange(inner)[None, :] % inner * (2.0 * math.pi / inner)
    parity = []
    for e in range(2):
        ic, isn = np.cos(angles[:, e::2]), np.sin(angles[:, e::2])
        parity.append((np.block([[ic, -isn], [isn, ic]]), np.block([[ic.T, isn.T], [-isn.T, ic.T]])))
    w2 = np.stack(split(np.stack([pair[0] for pair in parity])))
    v2 = split(np.stack([pair[1] for pair in parity]))[0]
    v1 = split(np.block([[oc, -osn], [osn, oc]]))[0]
    twist = twiddles(outer, inner)
    signal = (
        echoes.reshape(2, groups, GROUP, tiles, 128)
        .transpose(0, 1, 3, 2, 4)
        .reshape(2, groups, tiles * GROUP, 128)
    )
    response = doppler_filter.reshape(2, inner, outer).transpose(1, 0, 2).reshape(2 * inner, outer)
    hbm = pl.BlockSpec(memory_space=pltpu.HBM)
    vmem = pl.BlockSpec(memory_space=pltpu.VMEM)
    piece = (2, GROUP, CHUNK, inner)
    ints = (inner, outer)
    pin = lambda a: pltpu.with_memory_space_constraint(a, pltpu.HBM)
    y, v1_here = pl.pallas_call(
        functools.partial(main_kernel, count, outer, inner, taps),
        in_specs=[hbm] * 10,
        out_specs=[vmem, vmem],
        out_shape=[
            jax.ShapeDtypeStruct((rows, 2, outer, inner), bf16),
            jax.ShapeDtypeStruct(v1.shape, bf16),
        ],
        scratch_shapes=[
            pltpu.VMEM(signal.shape, f32),
            pltpu.VMEM(w1.shape, bf16),
            pltpu.VMEM(w2.shape, bf16),
            pltpu.VMEM(twist.shape, f32),
            pltpu.VMEM(response.shape, f32),
            pltpu.VMEM(v2.shape, bf16),
            pltpu.VMEM(ints, jnp.int32),
            pltpu.VMEM(ints, jnp.int32),
            pltpu.VMEM(kernel_taps.shape, f32),
            pltpu.VMEM((outer, inner), f32),
            pltpu.VMEM((outer, inner), f32),
            pltpu.VMEM((outer, inner), jnp.int32),
            pltpu.VMEM((outer, inner), jnp.int32),
            pltpu.VMEM((taps, 128), f32),
            pltpu.VMEM((groups, chunks) + piece, bf16),
            pltpu.VMEM((groups, chunks) + piece, bf16),
            pltpu.VMEM((chunks,) + piece, bf16),
            pltpu.VMEM((chunks,) + piece, bf16),
            pltpu.VMEM((chunks,) + piece, bf16),
            pltpu.VMEM((GROUP // 2, chunks, 2, 2, CHUNK, inner), bf16),
            pltpu.VMEM((rows, CHUNK, 2 * inner), f32),
            pltpu.SemaphoreType.DMA((2,)),
            pltpu.SemaphoreType.DMA((9,)),
            pltpu.SemaphoreType.DMA((9, 8)),
            pltpu.SemaphoreType.DMA((8, 8)),
        ],
        compiler_params=pltpu.CompilerParams(
            collective_id=0, has_side_effects=True, vmem_limit_bytes=40 << 20
        ),
        name="main",
    )(*(
        pin(jnp.asarray(a))
        for a in (
            signal, w1, w2, twist, response, v2, v1,
            migration_shift.reshape(ints), kernel_index.reshape(ints), kernel_taps,
        )
    ))
    image = pl.pallas_call(
        functools.partial(last_kernel, outer, inner),
        in_specs=[vmem, vmem],
        out_specs=hbm,
        out_shape=jax.ShapeDtypeStruct(signal.shape, f32),
        scratch_shapes=[pltpu.VMEM(signal.shape, f32), pltpu.SemaphoreType.DMA((groups,))],
        compiler_params=pltpu.CompilerParams(vmem_limit_bytes=40 << 20),
        name="last",
    )(v1_here, y)
    return (
        image.reshape(2, groups, tiles, GROUP, 128)
        .transpose(0, 1, 3, 2, 4)
        .reshape(2, rows, pulses)
    )


def solution(mesh):
    return jax.shard_map(
        per_device,
        mesh=mesh,
        in_specs=(P(None, ("swath", "rng"), None), P(), P(), P(), P()),
        out_specs=P(None, ("swath", "rng"), None),
        check_vma=False,
    )
```

```python
import functools
import math

import jax
import jax.numpy as jnp
import numpy as np
from jax import lax
from jax.experimental import pallas as pl
from jax.experimental.pallas import tpu as pltpu
from jax.sharding import PartitionSpec as P

F2 = 256
SMAX = 9
GROUP = 8
CHUNK = 16
HEAD = 4

f32 = jnp.float32
bf16 = jnp.bfloat16


MESH = pl.DeviceIdType.MESH


def dft(length):
    numbers = np.arange(length)
    angles = (numbers[:, None] * numbers[None, :] % length) * (2.0 * math.pi / length)
    return np.cos(angles), np.sin(angles)


def split(table):
    table = table.astype(np.float32)
    high = table.astype(bf16)
    return high, (table - high.astype(np.float32)).astype(bf16)


def twiddles(outer, inner):
    angles = (np.arange(outer)[:, None] * np.arange(inner)[None, :]) * (
        2.0 * math.pi / (outer * inner)
    )
    return np.stack([np.cos(angles), np.sin(angles)]).astype(np.float32)


def dot(a, b):
    return jnp.dot(a, b, preferred_element_type=f32)


def halves(value):
    high = value.astype(bf16)
    return high, (value - high.astype(f32)).astype(bf16)


def main_kernel(
    count, outer, inner, taps,
    x_hbm, w_hbm, t_hbm, h_hbm, v_hbm, s_hbm, k_hbm, taps_hbm,
    y_ref, v_ref,
    x_buf, w_ref, t_ref, h_ref, s_in, k_in, taps_ref,
    hr_ref, hi_ref, s_ref, k_ref, tab_ref, own, prev, nxt, low, mix, m_ref,
    lsem, ssem, rsem,
):
    me = lax.axis_index("rng")
    role = me % 4
    first = me < 4
    final = me >= count - 4
    lanes = 128
    parts = inner // lanes
    stride = GROUP * parts
    chunks = outer // CHUNK
    rows = 2 * GROUP
    lead = jnp.where(role == 0, 0, jnp.where(role == 2, 0, 1))

    def fetch(g):
        return pltpu.make_async_copy(x_hbm.at[:, g], x_buf.at[:, g], lsem.at[g])

    tables = [
        pltpu.make_async_copy(src, dst, lsem.at[2 + n])
        for n, (src, dst) in enumerate(
            (
                (h_hbm, h_ref),
                (w_hbm, w_ref),
                (t_hbm, t_ref),
                (s_hbm, s_in),
                (k_hbm, k_in),
                (taps_hbm, taps_ref),
                (v_hbm, v_ref),
            )
        )
    ]
    tables[0].start()
    fetch(lead).start()
    tables[1].start()
    tables[2].start()

    barrier = pltpu.get_barrier_semaphore()

    def greet(target):
        pl.semaphore_signal(barrier, inc=1, device_id={"rng": target}, device_id_type=MESH)

    @pl.when(role == 0)
    def _():
        greet(me + 1)

        @pl.when(jnp.logical_not(first))
        def _():
            greet(me - 1)
            greet(me - 3)

    @pl.when(role == 1)
    def _():
        greet(me - 1)
        greet(me + 1)

        @pl.when(jnp.logical_not(final))
        def _():
            greet(me + 3)

    @pl.when(role == 2)
    def _():
        greet(me - 1)
        greet(me + 1)

    @pl.when(role == 3)
    def _():
        greet(me - 1)

        @pl.when(jnp.logical_not(final))
        def _():
            greet(me + 1)

    norm = 1.0 / math.sqrt(outer * inner)
    tables[0].wait()
    for e in range(2):
        here = pl.ds(e * lanes, lanes)
        hr_ref[:, here] = h_ref[pl.ds(e * 2, lanes, stride=4), :].T * norm
        hi_ref[:, here] = h_ref[pl.ds(e * 2 + 1, lanes, stride=4), :].T * norm
    tables[1].wait()
    tables[2].wait()

    def second(n, e):
        return w_ref[pl.ds(4 * outer + (2 * n + e) * inner, inner), :]

    batches = (
        (lead, 0, 2),
        (lead, 2, 2),
        (jnp.where(role == 3, 0, lead), jnp.where(role == 3, 0, 4), 4),
        (jnp.where(role == 3, 0, 1 - lead), jnp.where(role == 3, 4, 0), 4),
        (jnp.where(role == 3, 1, 1 - lead), 4, 4),
    )

    def forward(g, first_row, n):
        sums = [([], []), ([], [])]
        for j in range(n):
            r = first_row + j
            columns = []
            for c in range(2):
                columns.append(
                    jnp.concatenate(
                        [
                            x_buf[c, g, pl.ds(h * GROUP + r, outer, stride=stride), :]
                            for h in range(parts)
                        ],
                        axis=1,
                    )
                )
            xh, xl = halves(jnp.concatenate(columns, axis=0))
            both = dot(w_ref[: 4 * outer, :], xh)
            s = both[: 2 * outer] + dot(w_ref[: 2 * outer, :], xl) + both[2 * outer :]
            re, im = s[:outer], s[outer:]
            tc, ts = t_ref[0], t_ref[1]
            re, im = re * tc + im * ts, im * tc - re * ts
            left = jnp.concatenate([re[:, :lanes], im[:, :lanes]], axis=1)
            right = jnp.concatenate([re[:, lanes:], im[:, lanes:]], axis=1)
            for e, value in enumerate((left + right, left - right)):
                a, b = halves(value)
                sums[e][0].append(a)
                sums[e][1].append(b)
        for e in range(2):
            both = dot(jnp.concatenate(sums[e][0] + sums[e][1], axis=0), second(0, e))
            high = jnp.concatenate(sums[e][0], axis=0)
            z = both[: n * outer] + dot(high, second(1, e)) + both[n * outer :]
            here = pl.ds(e * lanes, lanes)
            hr, hi = hr_ref[:, here], hi_ref[:, here]
            for j in range(n):
                re = z[j * outer : (j + 1) * outer, :lanes]
                im = z[j * outer : (j + 1) * outer, lanes:]
                own[g, :, 0, first_row + j, :, here] = (re * hr + im * hi).astype(bf16).reshape(chunks, CHUNK, lanes)
                own[g, :, 1, first_row + j, :, here] = (im * hr - re * hi).astype(bf16).reshape(chunks, CHUNK, lanes)

    def copy(src, dst, sent, got, target):
        return pltpu.make_async_remote_copy(
            src_ref=src,
            dst_ref=dst,
            send_sem=ssem.at[sent],
            recv_sem=rsem.at[got],
            device_id={"rng": target % count},
            device_id_type=MESH,
        )

    def some(ref, g, first_row, n):
        return ref.at[g, :, :, pl.ds(first_row, n)]

    def rows_down(g, first_row, n):
        return copy(some(own, g, first_row, n), some(prev, g, first_row, n), 0, 0, me + 1)

    def all_down():
        return copy(own, prev, 0, 0, me + 1)

    def up(first_row, n):
        part = (slice(None), slice(None), pl.ds(first_row, n))
        return copy(own.at[(0,) + part], nxt.at[part], 1, 1, me + count - 1)

    def far_up(c):
        return copy(own.at[0, c], low.at[c], 1, 2 + chunks + c, me + count - 3)

    def mix_down(c):
        return copy(mix.at[c], prev.at[0, c], 2, 2 + c, me + 1)

    def mix_up(c):
        return copy(mix.at[c], nxt.at[c], 2, 2 + c, me + count - 1)

    def tail_down(c):
        part = (1, c, slice(None), pl.ds(HEAD, GROUP - HEAD))
        return copy(own.at[part], prev.at[part], 2, 2 + chunks + c, me + 1)

    def relay_down(c):
        return copy(nxt.at[c], prev.at[0, c], 3, 2 + c, me + 3)

    def relay_up(c):
        return copy(prev.at[0, c], nxt.at[c], 3, 2 + c, me + 1)

    fetch(lead).wait()
    fetch(1 - lead).start()
    for n in range(3, 7):
        tables[n].start()

    def send(g, first_row, n):
        @pl.when((role == 0) | (role == 2) | ((role == 1) & (g == 1)))
        def _():
            rows_down(g, first_row, n).start()

        @pl.when((role == 3) & jnp.logical_not(final) & (g == 1) & (first_row < HEAD))
        def _():
            rows_down(g, first_row, n).start()

        @pl.when(((role == 1) | (role == 3)) & (g == 0))
        def _():
            up(first_row, n).start()

        @pl.when((g == 0) & (first_row + n == GROUP) & (role == 0) & jnp.logical_not(first))
        def _():
            for c in range(chunks):
                far_up(c).start()

    for i, batch in enumerate(batches):
        if i == 2 or i == 3:

            @pl.when((role == 3) == (i == 2))
            def _():
                fetch(1 - lead).wait()

        forward(*batch)
        if i == 0:
            for amount, here in (
                (1, ((role == 0) & first) | ((role == 3) & final)),
                (2, (role == 2) | ((role == 1) & final) | ((role == 3) & jnp.logical_not(final))),
                (3, ((role == 0) & jnp.logical_not(first)) | ((role == 1) & jnp.logical_not(final))),
            ):

                @pl.when(here)
                def _():
                    pl.semaphore_wait(barrier, amount)

        send(*batch)
    for n in range(3, 7):
        tables[n].wait()
    for e in range(2):
        here = pl.ds(e * lanes, lanes)
        s_ref[:, here] = s_in[pl.ds(e, lanes, stride=2), :].T
        k_ref[:, here] = k_in[pl.ds(e, lanes, stride=2), :].T
    padded = jnp.concatenate([taps_ref[...], jnp.zeros((taps_ref.shape[0], lanes - taps), f32)], axis=1)
    padded = jnp.concatenate([padded, jnp.zeros((lanes - taps_ref.shape[0], lanes), f32)], axis=0)
    tab_ref[...] = padded.T[:taps]

    def merge(c, high, lower):
        limit = SMAX - s_ref[pl.ds(pl.multiple_of(c * CHUNK, CHUNK), CHUNK), :]
        for d in range(2):
            for j in range(GROUP):
                mix[c, d, j] = jnp.where(
                    limit <= j, high[c, d, j].astype(f32), lower[c, d, j].astype(f32)
                ).astype(bf16)

    def send_mix(c):
        @pl.when(jnp.logical_not(final))
        def _():
            far_up(c).wait_recv()

        merge(c, own.at[0], low)
        mix_down(c).start()

    @pl.when((role == 0) & first)
    def _():
        prev[...] = jnp.zeros_like(prev)

    @pl.when((role == 1) & final)
    def _():
        low[...] = jnp.zeros_like(low)

    ahead = 2
    pace = (0, 0, 1, 2, 3, 4, 5, 6)

    @pl.when((role == 0) & jnp.logical_not(first))
    def _():
        rows_down(1, 0, HEAD).wait_recv()

    @pl.when(role == 1)
    def _():
        def head(c, _):
            send_mix(c)
            return 0

        lax.fori_loop(0, ahead, head, 0)

    @pl.when((role == 1) | (role == 3))
    def _():
        all_down().wait_recv()

    @pl.when((role == 0) | (role == 2))
    def _():
        up(0, GROUP).wait_recv()

    @pl.when(role == 2)
    def _():
        def head(c, _):
            merge(c, nxt, own.at[0])
            mix_up(c).start()
            return 0

        lax.fori_loop(0, chunks, head, 0)
        rows_down(1, 0, GROUP).wait_recv()

    def migrate(c):
        base = pl.multiple_of(c * CHUNK, CHUNK)
        for sub in range(CHUNK // 8):
            for part in range(parts):
                a = slice(sub * 8, sub * 8 + 8)
                b = slice(part * lanes, part * lanes + lanes)
                offset = SMAX - s_ref[pl.ds(base + sub * 8, 8), b]
                which = k_ref[pl.ds(base + sub * 8, 8), b]
                bits = [(offset & bit) != 0 for bit in (8, 4, 2, 1)]
                weights = [
                    jnp.take_along_axis(jnp.broadcast_to(tab_ref[k : k + 1, :], (8, 128)), which, axis=1, mode="promise_in_bounds")
                    for k in range(taps)
                ]
                for d in range(2):
                    line = [prev[g, c, d, i, a, b] for g in range(2) for i in range(GROUP)]
                    line += [own[g, c, d, i, a, b] for g in range(2) for i in range(GROUP)]
                    line += [nxt[c, d, i, a, b] for i in range(GROUP)]
                    line = [v.astype(f32) for v in line]
                    need = rows + taps - 1
                    for n, bit in enumerate((8, 4, 2, 1)):
                        keep = need + (bit - 1)
                        line = [
                            jnp.where(bits[n], line[j + bit], line[j]) if j + bit < len(line) else line[j]
                            for j in range(keep)
                        ]
                    for i in range(rows):
                        total = weights[0] * line[i + taps - 1]
                        for k in range(1, taps):
                            total = total + weights[k] * line[i + taps - 1 - k]
                        m_ref[i, a, part * inner + d * lanes : part * inner + d * lanes + lanes] = total
        flat = m_ref[...].reshape(rows * CHUNK, 2 * inner).astype(bf16)
        even = dot(flat[:, :inner], v_ref[:inner, :])
        odd = dot(flat[:, inner:], v_ref[inner : 2 * inner, :])
        here = pl.ds(base, CHUNK)
        for n, z in enumerate((even + odd, even - odd)):
            z = z.reshape(rows, CHUNK, inner)
            re, im = z[:, :, :lanes], z[:, :, lanes:]
            half = pl.ds(n * lanes, lanes)
            tc, ts = (t_ref[0, here, half] * norm)[None], (t_ref[1, here, half] * norm)[None]
            y_ref[:, 0, here, half] = (re * tc - im * ts).astype(bf16)
            y_ref[:, 1, here, half] = (re * ts + im * tc).astype(bf16)

    def work(c, _):
        @pl.when((role == 0) & jnp.logical_not(first))
        def _():
            tail_down(c).wait_recv()
            relay_down(c).wait_recv()

        @pl.when(role == 1)
        def _():
            @pl.when(c + ahead < chunks)
            def _():
                send_mix(c + ahead)

            mix_up(c).wait_recv()

            @pl.when(jnp.logical_not(final))
            def _():
                relay_down(c).start()

        @pl.when(role == 2)
        def _():
            mix_down(c).wait_recv()
            relay_up(c).start()

        @pl.when(role == 3)
        def _():
            for n in range(chunks):

                @pl.when(jnp.logical_not(final) & (c == pace[n * 8 // chunks] * chunks // 8))
                def _():
                    tail_down(n).start()

            relay_up(c).wait_recv()

        migrate(c)
        return 0

    lax.fori_loop(0, chunks, work, 0)

    def sent(n, ref):
        copy(ref, ref, n, 0, me + 1).wait_send()

    @pl.when(role == 0)
    def _():
        sent(0, own)

        @pl.when(jnp.logical_not(first))
        def _():
            sent(1, own.at[0])

    @pl.when(role == 1)
    def _():
        sent(0, own.at[1])
        sent(1, own.at[0])
        sent(2, mix)

        @pl.when(jnp.logical_not(final))
        def _():
            sent(3, nxt)

    @pl.when(role == 2)
    def _():
        sent(0, own)
        sent(2, mix)
        sent(3, prev.at[0])

    @pl.when(role == 3)
    def _():
        sent(1, own.at[0])

        @pl.when(jnp.logical_not(final))
        def _():
            sent(0, some(own, 1, 0, HEAD))
            sent(2, some(own, 1, HEAD, GROUP - HEAD))


def last_kernel(outer, inner, v_ref, y_ref, o_hbm, o_buf, sem):
    lanes = 128
    parts = inner // lanes
    stride = GROUP * parts
    groups = y_ref.shape[0] // GROUP
    outs = []
    for g in range(groups):
        for c in range(2):
            for r in range(GROUP):
                z = dot(
                    v_ref[2 * inner + c * outer : 2 * inner + (c + 1) * outer, :],
                    y_ref[g * GROUP + r].reshape(2 * outer, inner),
                )
                for h in range(parts):
                    o_buf[c, g, pl.ds(h * GROUP + r, outer, stride=stride), :] = z[:, h * lanes : (h + 1) * lanes]
            outs.append(pltpu.make_async_copy(o_buf.at[c, g], o_hbm.at[c, g], sem.at[2 * g + c]))
            outs[-1].start()
    for out in outs:
        out.wait()


def per_device(echoes, doppler_filter, migration_shift, kernel_index, kernel_taps):
    rows = echoes.shape[1]
    pulses = echoes.shape[2]
    inner = F2
    outer = pulses // inner
    taps = kernel_taps.shape[1]
    groups = rows // GROUP
    tiles = pulses // 128
    chunks = outer // CHUNK
    count = lax.axis_size("rng")
    assert groups == 2 and count % 4 == 0
    half = inner // 2
    oc, osn = dft(outer)
    w1 = split(np.block([[oc, osn], [-osn, oc]]))
    angles = np.arange(half)[:, None] * np.arange(inner)[None, :] % inner * (2.0 * math.pi / inner)
    parity = []
    for e in range(2):
        ic, isn = np.cos(angles[:, e::2]), np.sin(angles[:, e::2])
        parity.append((np.block([[ic, -isn], [isn, ic]]), np.block([[ic.T, isn.T], [-isn.T, ic.T]])))
    w2 = split(np.concatenate([pair[0] for pair in parity]))
    w = np.concatenate(w1 + w2)
    v = np.concatenate([pair[1] for pair in parity] + [np.block([[oc, -osn], [osn, oc]])]).astype(np.float32).astype(bf16)
    twist = twiddles(outer, inner)
    signal = (
        echoes.reshape(2, groups, GROUP, tiles, 128)
        .transpose(0, 1, 3, 2, 4)
        .reshape(2, groups, tiles * GROUP, 128)
    )
    response = doppler_filter.reshape(2, inner, outer).transpose(1, 0, 2).reshape(2 * inner, outer)
    hbm = pl.BlockSpec(memory_space=pltpu.HBM)
    vmem = pl.BlockSpec(memory_space=pltpu.VMEM)
    piece = (2, GROUP, CHUNK, inner)
    ints = (inner, outer)
    pin = lambda a: pltpu.with_memory_space_constraint(a, pltpu.HBM)
    y, v_here = pl.pallas_call(
        functools.partial(main_kernel, count, outer, inner, taps),
        in_specs=[hbm] * 8,
        out_specs=[vmem, vmem],
        out_shape=[
            jax.ShapeDtypeStruct((rows, 2, outer, inner), bf16),
            jax.ShapeDtypeStruct(v.shape, bf16),
        ],
        scratch_shapes=[
            pltpu.VMEM(signal.shape, f32),
            pltpu.VMEM(w.shape, bf16),
            pltpu.VMEM(twist.shape, f32),
            pltpu.VMEM(response.shape, f32),
            pltpu.VMEM(ints, jnp.int32),
            pltpu.VMEM(ints, jnp.int32),
            pltpu.VMEM(kernel_taps.shape, f32),
            pltpu.VMEM((outer, inner), f32),
            pltpu.VMEM((outer, inner), f32),
            pltpu.VMEM((outer, inner), jnp.int32),
            pltpu.VMEM((outer, inner), jnp.int32),
            pltpu.VMEM((taps, 128), f32),
            pltpu.VMEM((groups, chunks) + piece, bf16),
            pltpu.VMEM((groups, chunks) + piece, bf16),
            pltpu.VMEM((chunks,) + piece, bf16),
            pltpu.VMEM((chunks,) + piece, bf16),
            pltpu.VMEM((chunks,) + piece, bf16),
            pltpu.VMEM((rows, CHUNK, 2 * inner), f32),
            pltpu.SemaphoreType.DMA((9,)),
            pltpu.SemaphoreType.DMA((4,)),
            pltpu.SemaphoreType.DMA((2 + 2 * chunks,)),
        ],
        compiler_params=pltpu.CompilerParams(
            collective_id=0, has_side_effects=True, vmem_limit_bytes=40 << 20
        ),
        name="main",
    )(*(
        pin(jnp.asarray(a))
        for a in (
            signal, w, twist, response, v,
            migration_shift.reshape(ints), kernel_index.reshape(ints), kernel_taps,
        )
    ))
    image = pl.pallas_call(
        functools.partial(last_kernel, outer, inner),
        in_specs=[vmem, vmem],
        out_specs=hbm,
        out_shape=jax.ShapeDtypeStruct(signal.shape, f32),
        scratch_shapes=[pltpu.VMEM(signal.shape, f32), pltpu.SemaphoreType.DMA((2 * groups,))],
        compiler_params=pltpu.CompilerParams(vmem_limit_bytes=40 << 20),
        name="last",
    )(v_here, y)
    return (
        image.reshape(2, groups, tiles, GROUP, 128)
        .transpose(0, 1, 3, 2, 4)
        .reshape(2, rows, pulses)
    )


def solution(mesh):
    return jax.shard_map(
        per_device,
        mesh=mesh,
        in_specs=(P(None, ("swath", "rng"), None), P(), P(), P(), P()),
        out_specs=P(None, ("swath", "rng"), None),
        check_vma=False,
    )
```

```python
import functools
import math

import jax
import jax.numpy as jnp
import numpy as np
from jax import lax
from jax.experimental import pallas as pl
from jax.experimental.pallas import tpu as pltpu
from jax.sharding import PartitionSpec as P

F2 = 256
SMAX = 9
GROUP = 8
CHUNK = 16
HEAD = 4

f32 = jnp.float32
bf16 = jnp.bfloat16


MESH = pl.DeviceIdType.MESH


def dft(length):
    numbers = np.arange(length)
    angles = (numbers[:, None] * numbers[None, :] % length) * (2.0 * math.pi / length)
    return np.cos(angles), np.sin(angles)


def split(table):
    table = table.astype(np.float32)
    high = table.astype(bf16)
    return high, (table - high.astype(np.float32)).astype(bf16)


def twiddles(outer, inner):
    angles = (np.arange(outer)[:, None] * np.arange(inner)[None, :]) * (
        2.0 * math.pi / (outer * inner)
    )
    return np.stack([np.cos(angles), np.sin(angles)]).astype(np.float32)


def dot(a, b):
    return jnp.dot(a, b, preferred_element_type=f32)


def halves(value):
    high = value.astype(bf16)
    return high, (value - high.astype(f32)).astype(bf16)


def main_kernel(
    count, outer, inner, taps,
    x_hbm, w_hbm, t_hbm, h_hbm, v_hbm, s_hbm, k_hbm, taps_hbm,
    y_ref, v_ref,
    x_buf, w_ref, t_ref, h_ref, s_in, k_in, taps_ref,
    hr_ref, hi_ref, s_ref, k_ref, tab_ref, span, low, mix, m_ref,
    lsem, ssem, rsem,
):
    me = lax.axis_index("rng")
    role = me % 4
    first = me < 4
    final = me >= count - 4
    lanes = 128
    parts = inner // lanes
    stride = GROUP * parts
    chunks = outer // CHUNK
    rows = 2 * GROUP
    prev, own, nxt = span.at[pl.ds(0, 2)], span.at[pl.ds(2, 2)], span.at[4]
    lead = jnp.where(role == 0, 0, jnp.where(role == 2, 0, 1))

    def fetch(g):
        return pltpu.make_async_copy(x_hbm.at[:, g], x_buf.at[:, g], lsem.at[g])

    tables = [
        pltpu.make_async_copy(src, dst, lsem.at[2 + n])
        for n, (src, dst) in enumerate(
            (
                (h_hbm, h_ref),
                (w_hbm, w_ref),
                (t_hbm, t_ref),
                (s_hbm, s_in),
                (k_hbm, k_in),
                (taps_hbm, taps_ref),
                (v_hbm, v_ref),
            )
        )
    ]
    tables[0].start()
    fetch(lead).start()
    tables[1].start()
    tables[2].start()

    barrier = pltpu.get_barrier_semaphore()

    def greet(target):
        pl.semaphore_signal(barrier, inc=1, device_id={"rng": target}, device_id_type=MESH)

    @pl.when(role == 0)
    def _():
        greet(me + 1)

        @pl.when(jnp.logical_not(first))
        def _():
            greet(me - 1)
            greet(me - 3)

    @pl.when(role == 1)
    def _():
        greet(me - 1)
        greet(me + 1)

        @pl.when(jnp.logical_not(final))
        def _():
            greet(me + 3)

    @pl.when(role == 2)
    def _():
        greet(me - 1)
        greet(me + 1)

    @pl.when(role == 3)
    def _():
        greet(me - 1)

        @pl.when(jnp.logical_not(final))
        def _():
            greet(me + 1)

    norm = 1.0 / math.sqrt(outer * inner)
    tables[0].wait()
    for e in range(2):
        here = pl.ds(e * lanes, lanes)
        hr_ref[:, here] = h_ref[pl.ds(e * 2, lanes, stride=4), :].T * norm
        hi_ref[:, here] = h_ref[pl.ds(e * 2 + 1, lanes, stride=4), :].T * norm
    tables[1].wait()
    tables[2].wait()

    def second(n, e):
        return w_ref[pl.ds(4 * outer + (2 * n + e) * inner, inner), :]

    batches = (
        (lead, 0, 2),
        (lead, 2, 2),
        (jnp.where(role == 3, 0, lead), jnp.where(role == 3, 0, 4), 4),
        (jnp.where(role == 3, 0, 1 - lead), jnp.where(role == 3, 4, 0), 4),
        (jnp.where(role == 3, 1, 1 - lead), 4, 4),
    )

    def forward(g, first_row, n):
        sums = [([], []), ([], [])]
        for j in range(n):
            r = first_row + j
            columns = []
            for c in range(2):
                columns.append(
                    jnp.concatenate(
                        [
                            x_buf[c, g, pl.ds(h * GROUP + r, outer, stride=stride), :]
                            for h in range(parts)
                        ],
                        axis=1,
                    )
                )
            xh, xl = halves(jnp.concatenate(columns, axis=0))
            both = dot(w_ref[: 4 * outer, :], xh)
            s = both[: 2 * outer] + dot(w_ref[: 2 * outer, :], xl) + both[2 * outer :]
            re, im = s[:outer], s[outer:]
            tc, ts = t_ref[0], t_ref[1]
            re, im = re * tc + im * ts, im * tc - re * ts
            left = jnp.concatenate([re[:, :lanes], im[:, :lanes]], axis=1)
            right = jnp.concatenate([re[:, lanes:], im[:, lanes:]], axis=1)
            for e, value in enumerate((left + right, left - right)):
                a, b = halves(value)
                sums[e][0].append(a)
                sums[e][1].append(b)
        for e in range(2):
            both = dot(jnp.concatenate(sums[e][0] + sums[e][1], axis=0), second(0, e))
            high = jnp.concatenate(sums[e][0], axis=0)
            z = both[: n * outer] + dot(high, second(1, e)) + both[n * outer :]
            here = pl.ds(e * lanes, lanes)
            hr, hi = hr_ref[:, here], hi_ref[:, here]
            for j in range(n):
                re = z[j * outer : (j + 1) * outer, :lanes]
                im = z[j * outer : (j + 1) * outer, lanes:]
                own[g, :, 0, first_row + j, :, here] = (re * hr + im * hi).astype(bf16).reshape(chunks, CHUNK, lanes)
                own[g, :, 1, first_row + j, :, here] = (im * hr - re * hi).astype(bf16).reshape(chunks, CHUNK, lanes)

    def copy(src, dst, sent, got, target):
        return pltpu.make_async_remote_copy(
            src_ref=src,
            dst_ref=dst,
            send_sem=ssem.at[sent],
            recv_sem=rsem.at[got],
            device_id={"rng": target % count},
            device_id_type=MESH,
        )

    def some(ref, g, first_row, n):
        return ref.at[g, :, :, pl.ds(first_row, n)]

    def rows_down(g, first_row, n):
        return copy(some(own, g, first_row, n), some(prev, g, first_row, n), 0, 0, me + 1)

    def all_down():
        return copy(own, prev, 0, 0, me + 1)

    def up(first_row, n):
        part = (slice(None), slice(None), pl.ds(first_row, n))
        return copy(own.at[(0,) + part], nxt.at[part], 1, 1, me + count - 1)

    def far_up(c):
        return copy(own.at[0, c], low.at[c], 1, 2 + chunks + c, me + count - 3)

    def mix_down(c):
        return copy(mix.at[c], prev.at[0, c], 2, 2 + c, me + 1)

    def mix_up(c):
        return copy(mix.at[c], nxt.at[c], 2, 2 + c, me + count - 1)

    def tail_down(c):
        part = (1, c, slice(None), pl.ds(HEAD, GROUP - HEAD))
        return copy(own.at[part], prev.at[part], 2, 2 + chunks + c, me + 1)

    def relay_down(c):
        return copy(nxt.at[c], prev.at[0, c], 3, 2 + c, me + 3)

    def relay_up(c):
        return copy(prev.at[0, c], nxt.at[c], 3, 2 + c, me + 1)

    fetch(lead).wait()
    fetch(1 - lead).start()
    for n in range(3, 7):
        tables[n].start()

    def send(g, first_row, n):
        @pl.when((role == 0) | (role == 2) | ((role == 1) & (g == 1)))
        def _():
            rows_down(g, first_row, n).start()

        @pl.when((role == 3) & jnp.logical_not(final) & (g == 1) & (first_row < HEAD))
        def _():
            rows_down(g, first_row, n).start()

        @pl.when(((role == 1) | (role == 3)) & (g == 0))
        def _():
            up(first_row, n).start()

        @pl.when((g == 0) & (first_row + n == GROUP) & (role == 0) & jnp.logical_not(first))
        def _():
            for c in range(chunks):
                far_up(c).start()

    for i, batch in enumerate(batches):
        if i == 2 or i == 3:

            @pl.when((role == 3) == (i == 2))
            def _():
                fetch(1 - lead).wait()

        forward(*batch)
        if i == 0:
            for amount, here in (
                (1, ((role == 0) & first) | ((role == 3) & final)),
                (2, (role == 2) | ((role == 1) & final) | ((role == 3) & jnp.logical_not(final))),
                (3, ((role == 0) & jnp.logical_not(first)) | ((role == 1) & jnp.logical_not(final))),
            ):

                @pl.when(here)
                def _():
                    pl.semaphore_wait(barrier, amount)

        send(*batch)
    for n in range(3, 7):
        tables[n].wait()
    for e in range(2):
        here = pl.ds(e * lanes, lanes)
        s_ref[:, here] = s_in[pl.ds(e, lanes, stride=2), :].T
        k_ref[:, here] = k_in[pl.ds(e, lanes, stride=2), :].T
    padded = jnp.concatenate([taps_ref[...], jnp.zeros((taps_ref.shape[0], lanes - taps), f32)], axis=1)
    padded = jnp.concatenate([padded, jnp.zeros((lanes - taps_ref.shape[0], lanes), f32)], axis=0)
    tab_ref[...] = padded.T[:taps]

    def merge(c, high, lower):
        limit = SMAX - s_ref[pl.ds(pl.multiple_of(c * CHUNK, CHUNK), CHUNK), :]
        for d in range(2):
            for j in range(GROUP):
                mix[c, d, j] = jnp.where(
                    limit <= j, high[c, d, j].astype(f32), lower[c, d, j].astype(f32)
                ).astype(bf16)

    def send_mix(c):
        @pl.when(jnp.logical_not(final))
        def _():
            far_up(c).wait_recv()

        merge(c, own.at[0], low)
        mix_down(c).start()

    @pl.when((role == 0) & first)
    def _():
        prev[...] = jnp.zeros(prev.shape, bf16)

    @pl.when((role == 1) & final)
    def _():
        low[...] = jnp.zeros_like(low)

    ahead = 2
    pace = (0, 0, 0, 1, 3, 4, 5, 6)

    @pl.when((role == 0) & jnp.logical_not(first))
    def _():
        rows_down(1, 0, HEAD).wait_recv()

    @pl.when(role == 1)
    def _():
        def head(c, _):
            send_mix(c)
            return 0

        lax.fori_loop(0, ahead, head, 0)

    @pl.when((role == 1) | (role == 3))
    def _():
        all_down().wait_recv()

    @pl.when((role == 0) | (role == 2))
    def _():
        up(0, GROUP).wait_recv()

    @pl.when(role == 2)
    def _():
        def head(c, _):
            merge(c, nxt, own.at[0])
            mix_up(c).start()
            return 0

        lax.fori_loop(0, chunks, head, 0)
        rows_down(1, 0, GROUP).wait_recv()

    def migrate(c, half):
        base = pl.multiple_of(c * CHUNK, CHUNK)
        for sub in range(CHUNK // 8):
            for part in range(parts):
                a = slice(sub * 8, sub * 8 + 8)
                b = slice(part * lanes, part * lanes + lanes)
                offset = SMAX - s_ref[pl.ds(base + sub * 8, 8), b]
                which = k_ref[pl.ds(base + sub * 8, 8), b]
                bits = [(offset & bit) != 0 for bit in (8, 4, 2, 1)]
                weights = [
                    jnp.take_along_axis(jnp.broadcast_to(tab_ref[k : k + 1, :], (8, 128)), which, axis=1, mode="promise_in_bounds")
                    for k in range(taps)
                ]
                for d in range(2):
                    line = [span[half + g, c, d, i, a, b].astype(f32) for g in range(4) for i in range(GROUP)]
                    need = GROUP + taps - 1
                    for n, bit in enumerate((8, 4, 2, 1)):
                        keep = need + (bit - 1)
                        line = [
                            jnp.where(bits[n], line[j + bit], line[j]) if j + bit < len(line) else line[j]
                            for j in range(keep)
                        ]
                    for i in range(GROUP):
                        total = weights[0] * line[i + taps - 1]
                        for k in range(1, taps):
                            total = total + weights[k] * line[i + taps - 1 - k]
                        m_ref[half * GROUP + i, a, part * inner + d * lanes : part * inner + d * lanes + lanes] = total
    def restore(c):
        base = pl.multiple_of(c * CHUNK, CHUNK)
        flat = m_ref[...].reshape(rows * CHUNK, 2 * inner).astype(bf16)
        even = dot(flat[:, :inner], v_ref[:inner, :])
        odd = dot(flat[:, inner:], v_ref[inner : 2 * inner, :])
        here = pl.ds(base, CHUNK)
        for n, z in enumerate((even + odd, even - odd)):
            z = z.reshape(rows, CHUNK, inner)
            re, im = z[:, :, :lanes], z[:, :, lanes:]
            half = pl.ds(n * lanes, lanes)
            tc, ts = (t_ref[0, here, half] * norm)[None], (t_ref[1, here, half] * norm)[None]
            y_ref[:, 0, here, half] = (re * tc - im * ts).astype(bf16)
            y_ref[:, 1, here, half] = (re * ts + im * tc).astype(bf16)

    sooner = jnp.where((role == 0) | (role == 2), 1, 0)

    def work(c, _):
        @pl.when(role == 1)
        def _():
            @pl.when(c + ahead < chunks)
            def _():
                send_mix(c + ahead)

        @pl.when((role == 3) & jnp.logical_not(final))
        def _():
            for n in range(chunks):

                @pl.when(c == pace[n * 8 // chunks] * chunks // 8)
                def _():
                    tail_down(n).start()

        @pl.when((role == 0) & jnp.logical_not(first))
        def _():
            tail_down(c).wait_recv()

        def half(n, _):
            @pl.when((n == 1) & (role == 0) & jnp.logical_not(first))
            def _():
                relay_down(c).wait_recv()

            @pl.when((n == 1) & (role == 1))
            def _():
                mix_up(c).wait_recv()

                @pl.when(jnp.logical_not(final))
                def _():
                    relay_down(c).start()

            @pl.when((n == 1) & (role == 2))
            def _():
                mix_down(c).wait_recv()
                relay_up(c).start()

            @pl.when((n == 1) & (role == 3))
            def _():
                relay_up(c).wait_recv()

            migrate(c, jnp.where(n == 0, sooner, 1 - sooner))
            return 0

        lax.fori_loop(0, 2, half, 0)
        restore(c)
        return 0

    lax.fori_loop(0, chunks, work, 0)

    def sent(n, ref):
        copy(ref, ref, n, 0, me + 1).wait_send()

    @pl.when(role == 0)
    def _():
        sent(0, own)

        @pl.when(jnp.logical_not(first))
        def _():
            sent(1, own.at[0])

    @pl.when(role == 1)
    def _():
        sent(0, own.at[1])
        sent(1, own.at[0])
        sent(2, mix)

        @pl.when(jnp.logical_not(final))
        def _():
            sent(3, nxt)

    @pl.when(role == 2)
    def _():
        sent(0, own)
        sent(2, mix)
        sent(3, prev.at[0])

    @pl.when(role == 3)
    def _():
        sent(1, own.at[0])

        @pl.when(jnp.logical_not(final))
        def _():
            sent(0, some(own, 1, 0, HEAD))
            sent(2, some(own, 1, HEAD, GROUP - HEAD))


def last_kernel(outer, inner, v_ref, y_ref, o_hbm, o_buf, sem):
    lanes = 128
    parts = inner // lanes
    stride = GROUP * parts
    groups = y_ref.shape[0] // GROUP
    outs = []
    for g in range(groups):
        for c in range(2):
            for r in range(GROUP):
                z = dot(
                    v_ref[2 * inner + c * outer : 2 * inner + (c + 1) * outer, :],
                    y_ref[g * GROUP + r].reshape(2 * outer, inner),
                )
                for h in range(parts):
                    o_buf[c, g, pl.ds(h * GROUP + r, outer, stride=stride), :] = z[:, h * lanes : (h + 1) * lanes]
            outs.append(pltpu.make_async_copy(o_buf.at[c, g], o_hbm.at[c, g], sem.at[2 * g + c]))
            outs[-1].start()
    for out in outs:
        out.wait()


def per_device(echoes, doppler_filter, migration_shift, kernel_index, kernel_taps):
    rows = echoes.shape[1]
    pulses = echoes.shape[2]
    inner = F2
    outer = pulses // inner
    taps = kernel_taps.shape[1]
    groups = rows // GROUP
    tiles = pulses // 128
    chunks = outer // CHUNK
    count = lax.axis_size("rng")
    assert groups == 2 and count % 4 == 0
    half = inner // 2
    oc, osn = dft(outer)
    w1 = split(np.block([[oc, osn], [-osn, oc]]))
    angles = np.arange(half)[:, None] * np.arange(inner)[None, :] % inner * (2.0 * math.pi / inner)
    parity = []
    for e in range(2):
        ic, isn = np.cos(angles[:, e::2]), np.sin(angles[:, e::2])
        parity.append((np.block([[ic, -isn], [isn, ic]]), np.block([[ic.T, isn.T], [-isn.T, ic.T]])))
    w2 = split(np.concatenate([pair[0] for pair in parity]))
    w = np.concatenate(w1 + w2)
    v = np.concatenate([pair[1] for pair in parity] + [np.block([[oc, -osn], [osn, oc]])]).astype(np.float32).astype(bf16)
    twist = twiddles(outer, inner)
    signal = (
        echoes.reshape(2, groups, GROUP, tiles, 128)
        .transpose(0, 1, 3, 2, 4)
        .reshape(2, groups, tiles * GROUP, 128)
    )
    response = doppler_filter.reshape(2, inner, outer).transpose(1, 0, 2).reshape(2 * inner, outer)
    hbm = pl.BlockSpec(memory_space=pltpu.HBM)
    vmem = pl.BlockSpec(memory_space=pltpu.VMEM)
    piece = (2, GROUP, CHUNK, inner)
    ints = (inner, outer)
    pin = lambda a: pltpu.with_memory_space_constraint(a, pltpu.HBM)
    y, v_here = pl.pallas_call(
        functools.partial(main_kernel, count, outer, inner, taps),
        in_specs=[hbm] * 8,
        out_specs=[vmem, vmem],
        out_shape=[
            jax.ShapeDtypeStruct((rows, 2, outer, inner), bf16),
            jax.ShapeDtypeStruct(v.shape, bf16),
        ],
        scratch_shapes=[
            pltpu.VMEM(signal.shape, f32),
            pltpu.VMEM(w.shape, bf16),
            pltpu.VMEM(twist.shape, f32),
            pltpu.VMEM(response.shape, f32),
            pltpu.VMEM(ints, jnp.int32),
            pltpu.VMEM(ints, jnp.int32),
            pltpu.VMEM(kernel_taps.shape, f32),
            pltpu.VMEM((outer, inner), f32),
            pltpu.VMEM((outer, inner), f32),
            pltpu.VMEM((outer, inner), jnp.int32),
            pltpu.VMEM((outer, inner), jnp.int32),
            pltpu.VMEM((taps, 128), f32),
            pltpu.VMEM((2 * groups + 1, chunks) + piece, bf16),
            pltpu.VMEM((chunks,) + piece, bf16),
            pltpu.VMEM((chunks,) + piece, bf16),
            pltpu.VMEM((rows, CHUNK, 2 * inner), f32),
            pltpu.SemaphoreType.DMA((9,)),
            pltpu.SemaphoreType.DMA((4,)),
            pltpu.SemaphoreType.DMA((2 + 2 * chunks,)),
        ],
        compiler_params=pltpu.CompilerParams(
            collective_id=0, has_side_effects=True, vmem_limit_bytes=40 << 20
        ),
        name="main",
    )(*(
        pin(jnp.asarray(a))
        for a in (
            signal, w, twist, response, v,
            migration_shift.reshape(ints), kernel_index.reshape(ints), kernel_taps,
        )
    ))
    image = pl.pallas_call(
        functools.partial(last_kernel, outer, inner),
        in_specs=[vmem, vmem],
        out_specs=hbm,
        out_shape=jax.ShapeDtypeStruct(signal.shape, f32),
        scratch_shapes=[pltpu.VMEM(signal.shape, f32), pltpu.SemaphoreType.DMA((2 * groups,))],
        compiler_params=pltpu.CompilerParams(vmem_limit_bytes=40 << 20),
        name="last",
    )(v_here, y)
    return (
        image.reshape(2, groups, tiles, GROUP, 128)
        .transpose(0, 1, 3, 2, 4)
        .reshape(2, rows, pulses)
    )


def solution(mesh):
    return jax.shard_map(
        per_device,
        mesh=mesh,
        in_specs=(P(None, ("swath", "rng"), None), P(), P(), P(), P()),
        out_specs=P(None, ("swath", "rng"), None),
        check_vma=False,
    )
```

```python
import functools
import math

import jax
import jax.numpy as jnp
import numpy as np
from jax import lax
from jax.experimental import pallas as pl
from jax.experimental.pallas import tpu as pltpu
from jax.sharding import PartitionSpec as P

F2 = 256
SMAX = 9
GROUP = 8
CHUNK = 16
HEAD = 4

f32 = jnp.float32
bf16 = jnp.bfloat16


MESH = pl.DeviceIdType.MESH


def dft(length):
    numbers = np.arange(length)
    angles = (numbers[:, None] * numbers[None, :] % length) * (2.0 * math.pi / length)
    return np.cos(angles), np.sin(angles)


def split(table):
    table = table.astype(np.float32)
    high = table.astype(bf16)
    return high, (table - high.astype(np.float32)).astype(bf16)


def twiddles(outer, inner):
    angles = (np.arange(outer)[:, None] * np.arange(inner)[None, :]) * (
        2.0 * math.pi / (outer * inner)
    )
    return np.stack([np.cos(angles), np.sin(angles)]).astype(np.float32)


def dot(a, b):
    return jnp.dot(a, b, preferred_element_type=f32)


def halves(value):
    high = value.astype(bf16)
    return high, (value - high.astype(f32)).astype(bf16)


def main_kernel(
    count, outer, inner, taps,
    x_hbm, w_hbm, t_hbm, h_hbm, v_hbm, s_hbm, k_hbm, taps_hbm,
    y_ref, v_ref,
    x_buf, w_ref, t_ref, h_ref, s_in, k_in, taps_ref,
    hr_ref, hi_ref, s_ref, k_ref, tab_ref, span, low, mix, m_ref,
    lsem, ssem, rsem,
):
    me = lax.axis_index("rng")
    role = me % 4
    first = me < 4
    final = me >= count - 4
    lanes = 128
    parts = inner // lanes
    stride = GROUP * parts
    chunks = outer // CHUNK
    rows = 2 * GROUP
    prev, own, nxt = span.at[pl.ds(0, 2)], span.at[pl.ds(2, 2)], span.at[4]
    lead = jnp.where(role == 0, 0, jnp.where(role == 2, 0, 1))

    x_view = x_buf.reshape(2, 2, outer * parts, GROUP, lanes)

    def fetch(g):
        return pltpu.make_async_copy(x_hbm.at[:, g], x_view.at[:, g], lsem.at[g])

    def piece(n):
        here = (slice(None), lead, slice(None), pl.ds(n * 4, 4))
        return pltpu.make_async_copy(x_hbm.at[here], x_view.at[here], lsem.at[lead * (1 - n) + n * 9])

    tables = [
        pltpu.make_async_copy(src, dst, lsem.at[2 + n])
        for n, (src, dst) in enumerate(
            (
                (h_hbm, h_ref),
                (w_hbm, w_ref),
                (t_hbm, t_ref),
                (s_hbm, s_in),
                (k_hbm, k_in),
                (taps_hbm, taps_ref),
                (v_hbm, v_ref),
            )
        )
    ]
    tables[0].start()
    piece(0).start()
    tables[1].start()
    tables[2].start()

    barrier = pltpu.get_barrier_semaphore()

    def greet(target):
        pl.semaphore_signal(barrier, inc=1, device_id={"rng": target}, device_id_type=MESH)

    @pl.when(role == 0)
    def _():
        greet(me + 1)

        @pl.when(jnp.logical_not(first))
        def _():
            greet(me - 1)
            greet(me - 3)

    @pl.when(role == 1)
    def _():
        greet(me - 1)
        greet(me + 1)

        @pl.when(jnp.logical_not(final))
        def _():
            greet(me + 3)

    @pl.when(role == 2)
    def _():
        greet(me - 1)
        greet(me + 1)

    @pl.when(role == 3)
    def _():
        greet(me - 1)

        @pl.when(jnp.logical_not(final))
        def _():
            greet(me + 1)

    norm = 1.0 / math.sqrt(outer * inner)
    tables[0].wait()
    for e in range(2):
        here = pl.ds(e * lanes, lanes)
        hr_ref[:, here] = h_ref[pl.ds(e * 2, lanes, stride=4), :].T * norm
        hi_ref[:, here] = h_ref[pl.ds(e * 2 + 1, lanes, stride=4), :].T * norm
    tables[1].wait()
    tables[2].wait()

    def second(n, e):
        return w_ref[pl.ds(4 * outer + (2 * n + e) * inner, inner), :]

    batches = (
        (lead, 0, 2),
        (lead, 2, 2),
        (jnp.where(role == 3, 0, lead), jnp.where(role == 3, 0, 4), 4),
        (jnp.where(role == 3, 0, 1 - lead), jnp.where(role == 3, 4, 0), 4),
        (jnp.where(role == 3, 1, 1 - lead), 4, 4),
    )

    def forward(g, first_row, n):
        sums = [([], []), ([], [])]
        for j in range(n):
            r = first_row + j
            columns = []
            for c in range(2):
                columns.append(
                    jnp.concatenate(
                        [
                            x_buf[c, g, pl.ds(h * GROUP + r, outer, stride=stride), :]
                            for h in range(parts)
                        ],
                        axis=1,
                    )
                )
            xh, xl = halves(jnp.concatenate(columns, axis=0))
            both = dot(w_ref[: 4 * outer, :], xh)
            s = both[: 2 * outer] + dot(w_ref[: 2 * outer, :], xl) + both[2 * outer :]
            re, im = s[:outer], s[outer:]
            tc, ts = t_ref[0], t_ref[1]
            re, im = re * tc + im * ts, im * tc - re * ts
            left = jnp.concatenate([re[:, :lanes], im[:, :lanes]], axis=1)
            right = jnp.concatenate([re[:, lanes:], im[:, lanes:]], axis=1)
            for e, value in enumerate((left + right, left - right)):
                a, b = halves(value)
                sums[e][0].append(a)
                sums[e][1].append(b)
        for e in range(2):
            both = dot(jnp.concatenate(sums[e][0] + sums[e][1], axis=0), second(0, e))
            high = jnp.concatenate(sums[e][0], axis=0)
            z = both[: n * outer] + dot(high, second(1, e)) + both[n * outer :]
            here = pl.ds(e * lanes, lanes)
            hr, hi = hr_ref[:, here], hi_ref[:, here]
            for j in range(n):
                re = z[j * outer : (j + 1) * outer, :lanes]
                im = z[j * outer : (j + 1) * outer, lanes:]
                own[g, :, 0, first_row + j, :, here] = (re * hr + im * hi).astype(bf16).reshape(chunks, CHUNK, lanes)
                own[g, :, 1, first_row + j, :, here] = (im * hr - re * hi).astype(bf16).reshape(chunks, CHUNK, lanes)

    def copy(src, dst, sent, got, target):
        return pltpu.make_async_remote_copy(
            src_ref=src,
            dst_ref=dst,
            send_sem=ssem.at[sent],
            recv_sem=rsem.at[got],
            device_id={"rng": target % count},
            device_id_type=MESH,
        )

    def some(ref, g, first_row, n):
        return ref.at[g, :, :, pl.ds(first_row, n)]

    def rows_down(g, first_row, n):
        return copy(some(own, g, first_row, n), some(prev, g, first_row, n), 0, 0, me + 1)

    def all_down():
        return copy(own, prev, 0, 0, me + 1)

    def up(first_row, n):
        part = (slice(None), slice(None), pl.ds(first_row, n))
        return copy(own.at[(0,) + part], nxt.at[part], 1, 1, me + count - 1)

    def far_up(c):
        return copy(own.at[0, c], low.at[c], 1, 2 + chunks + c, me + count - 3)

    def mix_down(c):
        return copy(mix.at[c], prev.at[0, c], 2, 2 + c, me + 1)

    def mix_up(c, d):
        return copy(mix.at[c, d], nxt.at[c, d], 2, 2 + 2 * d * chunks + c, me + count - 1)

    def tail_down(c):
        part = (1, c, slice(None), pl.ds(HEAD, GROUP - HEAD))
        return copy(own.at[part], prev.at[part], 2, 2 + chunks + c, me + 1)

    def relay_down(c, d):
        return copy(nxt.at[c, d], prev.at[0, c, d], 3, 2 + 2 * d * chunks + c, me + 3)

    def relay_up(c):
        return copy(prev.at[0, c], nxt.at[c], 3, 2 + c, me + 1)

    piece(0).wait()
    piece(1).start()
    fetch(1 - lead).start()
    for n in range(3, 7):
        tables[n].start()

    def send(g, first_row, n):
        @pl.when((role == 0) | (role == 2) | ((role == 1) & (g == 1)))
        def _():
            rows_down(g, first_row, n).start()

        @pl.when((role == 3) & jnp.logical_not(final) & (g == 1) & (first_row < HEAD))
        def _():
            rows_down(g, first_row, n).start()

        @pl.when(((role == 1) | (role == 3)) & (g == 0))
        def _():
            up(first_row, n).start()

        @pl.when((g == 0) & (first_row + n == GROUP) & (role == 0) & jnp.logical_not(first))
        def _():
            for c in range(chunks):
                far_up(c).start()

    for i, batch in enumerate(batches):
        if i == 2:
            piece(1).wait()
        if i == 2 or i == 3:

            @pl.when((role == 3) == (i == 2))
            def _():
                fetch(1 - lead).wait()

        forward(*batch)
        if i == 0:
            for amount, here in (
                (1, ((role == 0) & first) | ((role == 3) & final)),
                (2, (role == 2) | ((role == 1) & final) | ((role == 3) & jnp.logical_not(final))),
                (3, ((role == 0) & jnp.logical_not(first)) | ((role == 1) & jnp.logical_not(final))),
            ):

                @pl.when(here)
                def _():
                    pl.semaphore_wait(barrier, amount)

        send(*batch)
    for n in range(3, 7):
        tables[n].wait()
    for e in range(2):
        here = pl.ds(e * lanes, lanes)
        s_ref[:, here] = s_in[pl.ds(e, lanes, stride=2), :].T
        k_ref[:, here] = k_in[pl.ds(e, lanes, stride=2), :].T
    padded = jnp.concatenate([taps_ref[...], jnp.zeros((taps_ref.shape[0], lanes - taps), f32)], axis=1)
    padded = jnp.concatenate([padded, jnp.zeros((lanes - taps_ref.shape[0], lanes), f32)], axis=0)
    tab_ref[...] = padded.T[:taps]

    def merge(c, high, lower):
        limit = SMAX - s_ref[pl.ds(pl.multiple_of(c * CHUNK, CHUNK), CHUNK), :]
        for d in range(2):
            for j in range(GROUP):
                mix[c, d, j] = jnp.where(
                    limit <= j, high[c, d, j].astype(f32), lower[c, d, j].astype(f32)
                ).astype(bf16)

    def send_mix(c):
        @pl.when(jnp.logical_not(final))
        def _():
            far_up(c).wait_recv()

        merge(c, own.at[0], low)
        mix_down(c).start()

    @pl.when((role == 0) & first)
    def _():
        prev[...] = jnp.zeros(prev.shape, bf16)

    @pl.when((role == 1) & final)
    def _():
        low[...] = jnp.zeros_like(low)

    ahead = 2
    pace = (0, 0, 0, 1, 3, 4, 5, 6)

    @pl.when((role == 0) & jnp.logical_not(first))
    def _():
        rows_down(1, 0, HEAD).wait_recv()

    @pl.when(role == 1)
    def _():
        def head(c, _):
            send_mix(c)
            return 0

        lax.fori_loop(0, ahead, head, 0)

    @pl.when((role == 1) | (role == 3))
    def _():
        all_down().wait_recv()

    @pl.when((role == 0) | (role == 2))
    def _():
        up(0, GROUP).wait_recv()

    @pl.when(role == 2)
    def _():
        def head(c, _):
            merge(c, nxt, own.at[0])
            for d in range(2):
                mix_up(c, d).start()
            return 0

        lax.fori_loop(0, chunks, head, 0)
        rows_down(1, 0, GROUP).wait_recv()

    def migrate(c, half):
        base = pl.multiple_of(c * CHUNK, CHUNK)
        for sub in range(CHUNK // 8):
            for part in range(parts):
                a = slice(sub * 8, sub * 8 + 8)
                b = slice(part * lanes, part * lanes + lanes)
                offset = SMAX - s_ref[pl.ds(base + sub * 8, 8), b]
                which = k_ref[pl.ds(base + sub * 8, 8), b]
                bits = [(offset & bit) != 0 for bit in (8, 4, 2, 1)]
                weights = [
                    jnp.take_along_axis(jnp.broadcast_to(tab_ref[k : k + 1, :], (8, 128)), which, axis=1, mode="promise_in_bounds")
                    for k in range(taps)
                ]
                for d in range(2):
                    line = [span[half + g, c, d, i, a, b].astype(f32) for g in range(4) for i in range(GROUP)]
                    need = GROUP + taps - 1
                    for n, bit in enumerate((8, 4, 2, 1)):
                        keep = need + (bit - 1)
                        line = [
                            jnp.where(bits[n], line[j + bit], line[j]) if j + bit < len(line) else line[j]
                            for j in range(keep)
                        ]
                    for i in range(GROUP):
                        total = weights[0] * line[i + taps - 1]
                        for k in range(1, taps):
                            total = total + weights[k] * line[i + taps - 1 - k]
                        m_ref[half * GROUP + i, a, part * inner + d * lanes : part * inner + d * lanes + lanes] = total
    def restore(c):
        base = pl.multiple_of(c * CHUNK, CHUNK)
        flat = m_ref[...].reshape(rows * CHUNK, 2 * inner).astype(bf16)
        even = dot(flat[:, :inner], v_ref[:inner, :])
        odd = dot(flat[:, inner:], v_ref[inner : 2 * inner, :])
        here = pl.ds(base, CHUNK)
        for n, z in enumerate((even + odd, even - odd)):
            z = z.reshape(rows, CHUNK, inner)
            re, im = z[:, :, :lanes], z[:, :, lanes:]
            half = pl.ds(n * lanes, lanes)
            tc, ts = (t_ref[0, here, half] * norm)[None], (t_ref[1, here, half] * norm)[None]
            y_ref[:, 0, here, half] = (re * tc - im * ts).astype(bf16)
            y_ref[:, 1, here, half] = (re * ts + im * tc).astype(bf16)

    sooner = jnp.where((role == 0) | (role == 2), 1, 0)

    def work(c, _):
        @pl.when(role == 1)
        def _():
            @pl.when(c + ahead < chunks)
            def _():
                send_mix(c + ahead)

        @pl.when((role == 3) & jnp.logical_not(final))
        def _():
            for n in range(chunks):

                @pl.when(c == pace[n * 8 // chunks] * chunks // 8)
                def _():
                    tail_down(n).start()

        @pl.when((role == 0) & jnp.logical_not(first))
        def _():
            tail_down(c).wait_recv()

        def half(n, _):
            @pl.when((n == 1) & (role == 0) & jnp.logical_not(first))
            def _():
                for d in range(2):
                    relay_down(c, d).wait_recv()

            @pl.when((n == 1) & (role == 1))
            def _():
                for d in range(2):
                    mix_up(c, d).wait_recv()

                    @pl.when(jnp.logical_not(final))
                    def _():
                        relay_down(c, d).start()

            @pl.when((n == 1) & (role == 2))
            def _():
                mix_down(c).wait_recv()
                relay_up(c).start()

            @pl.when((n == 1) & (role == 3))
            def _():
                relay_up(c).wait_recv()

            migrate(c, jnp.where(n == 0, sooner, 1 - sooner))
            return 0

        lax.fori_loop(0, 2, half, 0)
        restore(c)
        return 0

    lax.fori_loop(0, chunks, work, 0)

    def sent(n, ref):
        copy(ref, ref, n, 0, me + 1).wait_send()

    @pl.when(role == 0)
    def _():
        sent(0, own)

        @pl.when(jnp.logical_not(first))
        def _():
            sent(1, own.at[0])

    @pl.when(role == 1)
    def _():
        sent(0, own.at[1])
        sent(1, own.at[0])
        sent(2, mix)

        @pl.when(jnp.logical_not(final))
        def _():
            sent(3, nxt)

    @pl.when(role == 2)
    def _():
        sent(0, own)
        sent(2, mix)
        sent(3, prev.at[0])

    @pl.when(role == 3)
    def _():
        sent(1, own.at[0])

        @pl.when(jnp.logical_not(final))
        def _():
            sent(0, some(own, 1, 0, HEAD))
            sent(2, some(own, 1, HEAD, GROUP - HEAD))


def last_kernel(outer, inner, v_ref, y_ref, o_hbm, o_buf, sem):
    lanes = 128
    parts = inner // lanes
    stride = GROUP * parts
    groups = y_ref.shape[0] // GROUP
    outs = []
    for g in range(groups):
        for c in range(2):
            for r in range(GROUP):
                z = dot(
                    v_ref[2 * inner + c * outer : 2 * inner + (c + 1) * outer, :],
                    y_ref[g * GROUP + r].reshape(2 * outer, inner),
                )
                for h in range(parts):
                    o_buf[c, g, pl.ds(h * GROUP + r, outer, stride=stride), :] = z[:, h * lanes : (h + 1) * lanes]
            outs.append(pltpu.make_async_copy(o_buf.at[c, g], o_hbm.at[c, g], sem.at[2 * g + c]))
            outs[-1].start()
    for out in outs:
        out.wait()


def per_device(echoes, doppler_filter, migration_shift, kernel_index, kernel_taps):
    rows = echoes.shape[1]
    pulses = echoes.shape[2]
    inner = F2
    outer = pulses // inner
    taps = kernel_taps.shape[1]
    groups = rows // GROUP
    tiles = pulses // 128
    chunks = outer // CHUNK
    count = lax.axis_size("rng")
    assert groups == 2 and count % 4 == 0
    half = inner // 2
    oc, osn = dft(outer)
    w1 = split(np.block([[oc, osn], [-osn, oc]]))
    angles = np.arange(half)[:, None] * np.arange(inner)[None, :] % inner * (2.0 * math.pi / inner)
    parity = []
    for e in range(2):
        ic, isn = np.cos(angles[:, e::2]), np.sin(angles[:, e::2])
        parity.append((np.block([[ic, -isn], [isn, ic]]), np.block([[ic.T, isn.T], [-isn.T, ic.T]])))
    w2 = split(np.concatenate([pair[0] for pair in parity]))
    w = np.concatenate(w1 + w2)
    v = np.concatenate([pair[1] for pair in parity] + [np.block([[oc, -osn], [osn, oc]])]).astype(np.float32).astype(bf16)
    twist = twiddles(outer, inner)
    signal = (
        echoes.reshape(2, groups, GROUP, tiles, 128)
        .transpose(0, 1, 3, 2, 4)
    )
    response = doppler_filter.reshape(2, inner, outer).transpose(1, 0, 2).reshape(2 * inner, outer)
    hbm = pl.BlockSpec(memory_space=pltpu.HBM)
    vmem = pl.BlockSpec(memory_space=pltpu.VMEM)
    piece = (2, GROUP, CHUNK, inner)
    ints = (inner, outer)
    pin = lambda a: pltpu.with_memory_space_constraint(a, pltpu.HBM)
    y, v_here = pl.pallas_call(
        functools.partial(main_kernel, count, outer, inner, taps),
        in_specs=[hbm] * 8,
        out_specs=[vmem, vmem],
        out_shape=[
            jax.ShapeDtypeStruct((rows, 2, outer, inner), bf16),
            jax.ShapeDtypeStruct(v.shape, bf16),
        ],
        scratch_shapes=[
            pltpu.VMEM((2, groups, tiles * GROUP, 128), f32),
            pltpu.VMEM(w.shape, bf16),
            pltpu.VMEM(twist.shape, f32),
            pltpu.VMEM(response.shape, f32),
            pltpu.VMEM(ints, jnp.int32),
            pltpu.VMEM(ints, jnp.int32),
            pltpu.VMEM(kernel_taps.shape, f32),
            pltpu.VMEM((outer, inner), f32),
            pltpu.VMEM((outer, inner), f32),
            pltpu.VMEM((outer, inner), jnp.int32),
            pltpu.VMEM((outer, inner), jnp.int32),
            pltpu.VMEM((taps, 128), f32),
            pltpu.VMEM((2 * groups + 1, chunks) + piece, bf16),
            pltpu.VMEM((chunks,) + piece, bf16),
            pltpu.VMEM((chunks,) + piece, bf16),
            pltpu.VMEM((rows, CHUNK, 2 * inner), f32),
            pltpu.SemaphoreType.DMA((10,)),
            pltpu.SemaphoreType.DMA((4,)),
            pltpu.SemaphoreType.DMA((2 + 3 * chunks,)),
        ],
        compiler_params=pltpu.CompilerParams(
            collective_id=0, has_side_effects=True, vmem_limit_bytes=40 << 20
        ),
        name="main",
    )(*(
        pin(jnp.asarray(a))
        for a in (
            signal, w, twist, response, v,
            migration_shift.reshape(ints), kernel_index.reshape(ints), kernel_taps,
        )
    ))
    image = pl.pallas_call(
        functools.partial(last_kernel, outer, inner),
        in_specs=[vmem, vmem],
        out_specs=hbm,
        out_shape=jax.ShapeDtypeStruct((2, groups, tiles * GROUP, 128), f32),
        scratch_shapes=[pltpu.VMEM((2, groups, tiles * GROUP, 128), f32), pltpu.SemaphoreType.DMA((2 * groups,))],
        compiler_params=pltpu.CompilerParams(vmem_limit_bytes=40 << 20),
        name="last",
    )(v_here, y)
    return (
        image.reshape(2, groups, tiles, GROUP, 128)
        .transpose(0, 1, 3, 2, 4)
        .reshape(2, rows, pulses)
    )


def solution(mesh):
    return jax.shard_map(
        per_device,
        mesh=mesh,
        in_specs=(P(None, ("swath", "rng"), None), P(), P(), P(), P()),
        out_specs=P(None, ("swath", "rng"), None),
        check_vma=False,
    )
```

```python
import functools
import math

import jax
import jax.numpy as jnp
import numpy as np
from jax import lax
from jax.experimental import pallas as pl
from jax.experimental.pallas import tpu as pltpu
from jax.sharding import PartitionSpec as P

F2 = 256
SMAX = 9
GROUP = 8
CHUNK = 16
HEAD = 4

f32 = jnp.float32
bf16 = jnp.bfloat16


MESH = pl.DeviceIdType.MESH


def dft(length):
    numbers = np.arange(length)
    angles = (numbers[:, None] * numbers[None, :] % length) * (2.0 * math.pi / length)
    return np.cos(angles), np.sin(angles)


def split(table):
    table = table.astype(np.float32)
    high = table.astype(bf16)
    return high, (table - high.astype(np.float32)).astype(bf16)


def twiddles(outer, inner):
    angles = (np.arange(outer)[:, None] * np.arange(inner)[None, :]) * (
        2.0 * math.pi / (outer * inner)
    )
    return np.stack([np.cos(angles), np.sin(angles)]).astype(np.float32)


def dot(a, b):
    return jnp.dot(a, b, preferred_element_type=f32)


def halves(value):
    high = value.astype(bf16)
    return high, (value - high.astype(f32)).astype(bf16)


def main_kernel(
    count, outer, inner, taps,
    x_hbm, w_hbm, t_hbm, h_hbm, v_hbm, s_hbm, k_hbm, taps_hbm,
    y_ref, v_ref,
    x_buf, w_ref, t_ref, h_ref, s_in, k_in, taps_ref,
    hr_ref, hi_ref, s_ref, k_ref, tab_ref, span, low, mix, m_ref,
    lsem, ssem, rsem,
):
    me = lax.axis_index("rng")
    role = me % 4
    first = me < 4
    final = me >= count - 4
    lanes = 128
    parts = inner // lanes
    stride = GROUP * parts
    chunks = outer // CHUNK
    rows = 2 * GROUP
    prev, own, nxt = span.at[pl.ds(0, 2)], span.at[pl.ds(2, 2)], span.at[4]
    lead = jnp.where(role == 0, 0, jnp.where(role == 2, 0, 1))

    x_view = x_buf.reshape(2, 2, outer * parts, GROUP, lanes)

    def fetch(g):
        return pltpu.make_async_copy(x_hbm.at[:, g], x_view.at[:, g], lsem.at[g])

    def piece(n):
        here = (slice(None), lead, slice(None), pl.ds(n * 4, 4))
        return pltpu.make_async_copy(x_hbm.at[here], x_view.at[here], lsem.at[lead * (1 - n) + n * 9])

    tables = [
        pltpu.make_async_copy(src, dst, lsem.at[2 + n])
        for n, (src, dst) in enumerate(
            (
                (h_hbm, h_ref),
                (w_hbm, w_ref),
                (t_hbm, t_ref),
                (s_hbm, s_in),
                (k_hbm, k_in),
                (taps_hbm, taps_ref),
                (v_hbm, v_ref),
            )
        )
    ]
    tables[0].start()
    piece(0).start()
    tables[1].start()
    tables[2].start()

    barrier = pltpu.get_barrier_semaphore()

    def greet(target):
        pl.semaphore_signal(barrier, inc=1, device_id={"rng": target}, device_id_type=MESH)

    @pl.when(role == 0)
    def _():
        greet(me + 1)

        @pl.when(jnp.logical_not(first))
        def _():
            greet(me - 1)
            greet(me - 3)

    @pl.when(role == 1)
    def _():
        greet(me - 1)
        greet(me + 1)

        @pl.when(jnp.logical_not(final))
        def _():
            greet(me + 3)

    @pl.when(role == 2)
    def _():
        greet(me - 1)
        greet(me + 1)

    @pl.when(role == 3)
    def _():
        greet(me - 1)

        @pl.when(jnp.logical_not(final))
        def _():
            greet(me + 1)

    norm = 1.0 / math.sqrt(outer * inner)
    tables[0].wait()
    for e in range(2):
        here = pl.ds(e * lanes, lanes)
        hr_ref[:, here] = h_ref[pl.ds(e * 2, lanes, stride=4), :].T * norm
        hi_ref[:, here] = h_ref[pl.ds(e * 2 + 1, lanes, stride=4), :].T * norm
    tables[1].wait()
    tables[2].wait()

    def second(n, e):
        return w_ref[pl.ds(4 * outer + (2 * n + e) * inner, inner), :]

    batches = (
        (lead, 0, 2),
        (lead, 2, 2),
        (jnp.where(role == 3, 0, lead), jnp.where(role == 3, 0, 4), 4),
        (jnp.where(role == 3, 0, 1 - lead), jnp.where(role == 3, 4, 0), 4),
        (jnp.where(role == 3, 1, 1 - lead), 4, 4),
    )

    def forward(g, first_row, n):
        sums = [([], []), ([], [])]
        for j in range(n):
            r = first_row + j
            columns = []
            for c in range(2):
                columns.append(
                    jnp.concatenate(
                        [
                            x_buf[c, g, pl.ds(h * GROUP + r, outer, stride=stride), :]
                            for h in range(parts)
                        ],
                        axis=1,
                    )
                )
            xh, xl = halves(jnp.concatenate(columns, axis=0))
            both = dot(w_ref[: 4 * outer, :], xh)
            s = both[: 2 * outer] + dot(w_ref[: 2 * outer, :], xl) + both[2 * outer :]
            re, im = s[:outer], s[outer:]
            tc, ts = t_ref[0], t_ref[1]
            re, im = re * tc + im * ts, im * tc - re * ts
            left = jnp.concatenate([re[:, :lanes], im[:, :lanes]], axis=1)
            right = jnp.concatenate([re[:, lanes:], im[:, lanes:]], axis=1)
            for e, value in enumerate((left + right, left - right)):
                a, b = halves(value)
                sums[e][0].append(a)
                sums[e][1].append(b)
        for e in range(2):
            both = dot(jnp.concatenate(sums[e][0] + sums[e][1], axis=0), second(0, e))
            high = jnp.concatenate(sums[e][0], axis=0)
            z = both[: n * outer] + dot(high, second(1, e)) + both[n * outer :]
            here = pl.ds(e * lanes, lanes)
            hr, hi = hr_ref[:, here], hi_ref[:, here]
            for j in range(n):
                re = z[j * outer : (j + 1) * outer, :lanes]
                im = z[j * outer : (j + 1) * outer, lanes:]
                own[g, :, 0, first_row + j, :, here] = (re * hr + im * hi).astype(bf16).reshape(chunks, CHUNK, lanes)
                own[g, :, 1, first_row + j, :, here] = (im * hr - re * hi).astype(bf16).reshape(chunks, CHUNK, lanes)

    def copy(src, dst, sent, got, target):
        return pltpu.make_async_remote_copy(
            src_ref=src,
            dst_ref=dst,
            send_sem=ssem.at[sent],
            recv_sem=rsem.at[got],
            device_id={"rng": target % count},
            device_id_type=MESH,
        )

    def some(ref, g, first_row, n):
        return ref.at[g, :, :, pl.ds(first_row, n)]

    def rows_down(g, first_row, n):
        return copy(some(own, g, first_row, n), some(prev, g, first_row, n), 0, 0, me + 1)

    def all_down():
        return copy(own, prev, 0, 0, me + 1)

    def up(first_row, n):
        part = (slice(None), slice(None), pl.ds(first_row, n))
        return copy(own.at[(0,) + part], nxt.at[part], 1, 1, me + count - 1)

    def far_up(c):
        return copy(own.at[0, c], low.at[c], 1, 2 + chunks + c, me + count - 3)

    def mix_down(c):
        return copy(mix.at[c], prev.at[0, c], 2, 2 + c, me + 1)

    def mix_up(c, d):
        return copy(mix.at[c, d], nxt.at[c, d], 2, 2 + 2 * d * chunks + c, me + count - 1)

    def tail_down(c):
        part = (1, c, slice(None), pl.ds(HEAD, GROUP - HEAD))
        return copy(own.at[part], prev.at[part], 2, 2 + chunks + c, me + 1)

    def relay_down(c, d):
        return copy(nxt.at[c, d], prev.at[0, c, d], 3, 2 + 2 * d * chunks + c, me + 3)

    def relay_up(c):
        return copy(prev.at[0, c], nxt.at[c], 3, 2 + c, me + 1)

    piece(0).wait()
    piece(1).start()
    fetch(1 - lead).start()
    for n in range(3, 7):
        tables[n].start()

    def send(g, first_row, n):
        @pl.when((role == 0) | (role == 2) | ((role == 1) & (g == 1)))
        def _():
            rows_down(g, first_row, n).start()

        @pl.when((role == 3) & jnp.logical_not(final) & (g == 1) & (first_row < HEAD))
        def _():
            rows_down(g, first_row, n).start()

        @pl.when(((role == 1) | (role == 3)) & (g == 0))
        def _():
            up(first_row, n).start()

        @pl.when((g == 0) & (first_row + n == GROUP) & (role == 0) & jnp.logical_not(first))
        def _():
            for c in range(chunks):
                far_up(c).start()

    for i, batch in enumerate(batches):
        if i == 2:
            piece(1).wait()
        if i == 2 or i == 3:

            @pl.when((role == 3) == (i == 2))
            def _():
                fetch(1 - lead).wait()

        if i == len(batches) - 1:
            for n in range(3, 7):
                tables[n].wait()
            for e in range(2):
                here = pl.ds(e * lanes, lanes)
                s_ref[:, here] = s_in[pl.ds(e, lanes, stride=2), :].T
                k_ref[:, here] = k_in[pl.ds(e, lanes, stride=2), :].T
            padded = jnp.concatenate([taps_ref[...], jnp.zeros((taps_ref.shape[0], lanes - taps), f32)], axis=1)
            padded = jnp.concatenate([padded, jnp.zeros((lanes - taps_ref.shape[0], lanes), f32)], axis=0)
            tab_ref[...] = padded.T[:taps]

        forward(*batch)
        if i == 0:
            for amount, here in (
                (1, ((role == 0) & first) | ((role == 3) & final)),
                (2, (role == 2) | ((role == 1) & final) | ((role == 3) & jnp.logical_not(final))),
                (3, ((role == 0) & jnp.logical_not(first)) | ((role == 1) & jnp.logical_not(final))),
            ):

                @pl.when(here)
                def _():
                    pl.semaphore_wait(barrier, amount)

        send(*batch)
    def merge(c, high, lower):
        limit = SMAX - s_ref[pl.ds(pl.multiple_of(c * CHUNK, CHUNK), CHUNK), :]
        for d in range(2):
            for j in range(GROUP):
                mix[c, d, j] = jnp.where(
                    limit <= j, high[c, d, j].astype(f32), lower[c, d, j].astype(f32)
                ).astype(bf16)

    def send_mix(c):
        @pl.when(jnp.logical_not(final))
        def _():
            far_up(c).wait_recv()

        merge(c, own.at[0], low)
        mix_down(c).start()

    @pl.when((role == 0) & first)
    def _():
        prev[...] = jnp.zeros(prev.shape, bf16)

    @pl.when((role == 1) & final)
    def _():
        low[...] = jnp.zeros_like(low)

    ahead = 2
    pace = (0, 0, 1, 2, 3, 4, 5, 6)

    @pl.when((role == 0) & jnp.logical_not(first))
    def _():
        rows_down(1, 0, HEAD).wait_recv()

    @pl.when(role == 1)
    def _():
        def head(c, _):
            send_mix(c)
            return 0

        lax.fori_loop(0, ahead, head, 0)

    @pl.when((role == 1) | (role == 3))
    def _():
        all_down().wait_recv()

    @pl.when((role == 0) | (role == 2))
    def _():
        up(0, GROUP).wait_recv()

    @pl.when(role == 2)
    def _():
        def head(c, _):
            merge(c, nxt, own.at[0])
            for d in range(2):
                mix_up(c, d).start()
            return 0

        lax.fori_loop(0, chunks, head, 0)
        rows_down(1, 0, GROUP).wait_recv()

    def migrate(c, half):
        base = pl.multiple_of(c * CHUNK, CHUNK)
        for sub in range(CHUNK // 8):
            for part in range(parts):
                a = slice(sub * 8, sub * 8 + 8)
                b = slice(part * lanes, part * lanes + lanes)
                offset = SMAX - s_ref[pl.ds(base + sub * 8, 8), b]
                which = k_ref[pl.ds(base + sub * 8, 8), b]
                bits = [(offset & bit) != 0 for bit in (8, 4, 2, 1)]
                weights = [
                    jnp.take_along_axis(jnp.broadcast_to(tab_ref[k : k + 1, :], (8, 128)), which, axis=1, mode="promise_in_bounds")
                    for k in range(taps)
                ]
                for d in range(2):
                    line = [span[half + g, c, d, i, a, b].astype(f32) for g in range(4) for i in range(GROUP)]
                    need = GROUP + taps - 1
                    for n, bit in enumerate((8, 4, 2, 1)):
                        keep = need + (bit - 1)
                        line = [
                            jnp.where(bits[n], line[j + bit], line[j]) if j + bit < len(line) else line[j]
                            for j in range(keep)
                        ]
                    for i in range(GROUP):
                        total = weights[0] * line[i + taps - 1]
                        for k in range(1, taps):
                            total = total + weights[k] * line[i + taps - 1 - k]
                        m_ref[half * GROUP + i, a, part * inner + d * lanes : part * inner + d * lanes + lanes] = total
    def restore(c):
        base = pl.multiple_of(c * CHUNK, CHUNK)
        flat = m_ref[...].reshape(rows * CHUNK, 2 * inner).astype(bf16)
        even = dot(flat[:, :inner], v_ref[:inner, :])
        odd = dot(flat[:, inner:], v_ref[inner : 2 * inner, :])
        here = pl.ds(base, CHUNK)
        for n, z in enumerate((even + odd, even - odd)):
            z = z.reshape(rows, CHUNK, inner)
            re, im = z[:, :, :lanes], z[:, :, lanes:]
            half = pl.ds(n * lanes, lanes)
            tc, ts = (t_ref[0, here, half] * norm)[None], (t_ref[1, here, half] * norm)[None]
            y_ref[:, 0, here, half] = (re * tc - im * ts).astype(bf16)
            y_ref[:, 1, here, half] = (re * ts + im * tc).astype(bf16)

    sooner = jnp.where((role == 0) | (role == 2), 1, 0)

    def work(c, _):
        @pl.when(role == 1)
        def _():
            @pl.when(c + ahead < chunks)
            def _():
                send_mix(c + ahead)

        @pl.when((role == 3) & jnp.logical_not(final))
        def _():
            for n in range(chunks):

                @pl.when(c == pace[n * 8 // chunks] * chunks // 8)
                def _():
                    tail_down(n).start()

        @pl.when((role == 0) & jnp.logical_not(first))
        def _():
            tail_down(c).wait_recv()

        def half(n, _):
            @pl.when((n == 1) & (role == 0) & jnp.logical_not(first))
            def _():
                for d in range(2):
                    relay_down(c, d).wait_recv()

            @pl.when((n == 1) & (role == 1))
            def _():
                for d in range(2):
                    mix_up(c, d).wait_recv()

                    @pl.when(jnp.logical_not(final))
                    def _():
                        relay_down(c, d).start()

            @pl.when((n == 1) & (role == 2))
            def _():
                mix_down(c).wait_recv()
                relay_up(c).start()

            @pl.when((n == 1) & (role == 3))
            def _():
                relay_up(c).wait_recv()

            migrate(c, jnp.where(n == 0, sooner, 1 - sooner))
            return 0

        lax.fori_loop(0, 2, half, 0)
        restore(c)
        return 0

    lax.fori_loop(0, chunks, work, 0)

    def sent(n, ref):
        copy(ref, ref, n, 0, me + 1).wait_send()

    @pl.when(role == 0)
    def _():
        sent(0, own)

        @pl.when(jnp.logical_not(first))
        def _():
            sent(1, own.at[0])

    @pl.when(role == 1)
    def _():
        sent(0, own.at[1])
        sent(1, own.at[0])
        sent(2, mix)

        @pl.when(jnp.logical_not(final))
        def _():
            sent(3, nxt)

    @pl.when(role == 2)
    def _():
        sent(0, own)
        sent(2, mix)
        sent(3, prev.at[0])

    @pl.when(role == 3)
    def _():
        sent(1, own.at[0])

        @pl.when(jnp.logical_not(final))
        def _():
            sent(0, some(own, 1, 0, HEAD))
            sent(2, some(own, 1, HEAD, GROUP - HEAD))


def last_kernel(outer, inner, v_ref, y_ref, o_hbm, o_buf, sem):
    lanes = 128
    parts = inner // lanes
    stride = GROUP * parts
    groups = y_ref.shape[0] // GROUP
    outs = []
    for g in range(groups):
        for c in range(2):
            for r in range(GROUP):
                z = dot(
                    v_ref[2 * inner + c * outer : 2 * inner + (c + 1) * outer, :],
                    y_ref[g * GROUP + r].reshape(2 * outer, inner),
                )
                for h in range(parts):
                    o_buf[c, g, pl.ds(h * GROUP + r, outer, stride=stride), :] = z[:, h * lanes : (h + 1) * lanes]
            outs.append(pltpu.make_async_copy(o_buf.at[c, g], o_hbm.at[c, g], sem.at[2 * g + c]))
            outs[-1].start()
    for out in outs:
        out.wait()


def per_device(echoes, doppler_filter, migration_shift, kernel_index, kernel_taps):
    rows = echoes.shape[1]
    pulses = echoes.shape[2]
    inner = F2
    outer = pulses // inner
    taps = kernel_taps.shape[1]
    groups = rows // GROUP
    tiles = pulses // 128
    chunks = outer // CHUNK
    count = lax.axis_size("rng")
    assert groups == 2 and count % 4 == 0
    half = inner // 2
    oc, osn = dft(outer)
    w1 = split(np.block([[oc, osn], [-osn, oc]]))
    angles = np.arange(half)[:, None] * np.arange(inner)[None, :] % inner * (2.0 * math.pi / inner)
    parity = []
    for e in range(2):
        ic, isn = np.cos(angles[:, e::2]), np.sin(angles[:, e::2])
        parity.append((np.block([[ic, -isn], [isn, ic]]), np.block([[ic.T, isn.T], [-isn.T, ic.T]])))
    w2 = split(np.concatenate([pair[0] for pair in parity]))
    w = np.concatenate(w1 + w2)
    v = np.concatenate([pair[1] for pair in parity] + [np.block([[oc, -osn], [osn, oc]])]).astype(np.float32).astype(bf16)
    twist = twiddles(outer, inner)
    signal = (
        echoes.reshape(2, groups, GROUP, tiles, 128)
        .transpose(0, 1, 3, 2, 4)
    )
    response = doppler_filter.reshape(2, inner, outer).transpose(1, 0, 2).reshape(2 * inner, outer)
    hbm = pl.BlockSpec(memory_space=pltpu.HBM)
    vmem = pl.BlockSpec(memory_space=pltpu.VMEM)
    piece = (2, GROUP, CHUNK, inner)
    ints = (inner, outer)
    pin = lambda a: pltpu.with_memory_space_constraint(a, pltpu.HBM)
    y, v_here = pl.pallas_call(
        functools.partial(main_kernel, count, outer, inner, taps),
        in_specs=[hbm] * 8,
        out_specs=[vmem, vmem],
        out_shape=[
            jax.ShapeDtypeStruct((rows, 2, outer, inner), bf16),
            jax.ShapeDtypeStruct(v.shape, bf16),
        ],
        scratch_shapes=[
            pltpu.VMEM((2, groups, tiles * GROUP, 128), f32),
            pltpu.VMEM(w.shape, bf16),
            pltpu.VMEM(twist.shape, f32),
            pltpu.VMEM(response.shape, f32),
            pltpu.VMEM(ints, jnp.int32),
            pltpu.VMEM(ints, jnp.int32),
            pltpu.VMEM(kernel_taps.shape, f32),
            pltpu.VMEM((outer, inner), f32),
            pltpu.VMEM((outer, inner), f32),
            pltpu.VMEM((outer, inner), jnp.int32),
            pltpu.VMEM((outer, inner), jnp.int32),
            pltpu.VMEM((taps, 128), f32),
            pltpu.VMEM((2 * groups + 1, chunks) + piece, bf16),
            pltpu.VMEM((chunks,) + piece, bf16),
            pltpu.VMEM((chunks,) + piece, bf16),
            pltpu.VMEM((rows, CHUNK, 2 * inner), f32),
            pltpu.SemaphoreType.DMA((10,)),
            pltpu.SemaphoreType.DMA((4,)),
            pltpu.SemaphoreType.DMA((2 + 3 * chunks,)),
        ],
        compiler_params=pltpu.CompilerParams(
            collective_id=0, has_side_effects=True, vmem_limit_bytes=40 << 20
        ),
        name="main",
    )(*(
        pin(jnp.asarray(a))
        for a in (
            signal, w, twist, response, v,
            migration_shift.reshape(ints), kernel_index.reshape(ints), kernel_taps,
        )
    ))
    image = pl.pallas_call(
        functools.partial(last_kernel, outer, inner),
        in_specs=[vmem, vmem],
        out_specs=hbm,
        out_shape=jax.ShapeDtypeStruct((2, groups, tiles * GROUP, 128), f32),
        scratch_shapes=[pltpu.VMEM((2, groups, tiles * GROUP, 128), f32), pltpu.SemaphoreType.DMA((2 * groups,))],
        compiler_params=pltpu.CompilerParams(vmem_limit_bytes=40 << 20),
        name="last",
    )(v_here, y)
    return (
        image.reshape(2, groups, tiles, GROUP, 128)
        .transpose(0, 1, 3, 2, 4)
        .reshape(2, rows, pulses)
    )


def solution(mesh):
    return jax.shard_map(
        per_device,
        mesh=mesh,
        in_specs=(P(None, ("swath", "rng"), None), P(), P(), P(), P()),
        out_specs=P(None, ("swath", "rng"), None),
        check_vma=False,
    )
```
